32 devices in a mesh: gz: 8 (over z, x), gy: 4 (over y, core).
Axes of the slice: x: 2, y: 2, z: 4, core: 2. Of those that a mesh axis runs over, the one named last changes fastest.
Arguments:
- features: bfloat16 [8, 4, 1, 64, 512], P('gz', 'gy'), may hold values from -6 to 6
- cotangent: bfloat16 [8, 4, 1, 64, 512], P('gz', 'gy'), may hold values from -6 to 6
- first_weight: bfloat16 [64, 1728], replicated, may hold values from -0.15625 to 0.15625
- second_weight: bfloat16 [64, 1728], replicated, may hold values from -0.15625 to 0.15625
- positions: int32 [8, 4, 1], P('gz', 'gy'), may hold values from 0 to 3, as said below
- counts: int32 [8, 4], P('gz', 'gy'), may hold values from 1 to 1, as said below
Outputs:
- output: bfloat16 [8, 4, 1, 64, 512], P('gz', 'gy')
- input_grad: bfloat16 [8, 4, 1, 64, 512], P('gz', 'gy')
- first_grad: float32 [64, 1728], replicated
- second_grad: float32 [64, 1728], replicated
The draws below stay inside these ranges and needn't reach their ends.
Inputs may be any that keep to these rules, and one draw needn't show every extreme that they name: The first counts[i, j] positions of each device are distinct. `counts`: some device has all 1 slots active.
All inputs are finite; a program needn't handle non-finite values.
Results may differ from the reference program's by a relative error of at most 0.0052.
Values may be sent and summed in bfloat16 or wider, within the bound.
A program may use at most 64 MiB of HBM per device.

```python
import math
import jax
import jax.numpy as jnp
from jax import lax

C = 64
E = 8
BY = 2
BX = 2
SLOTS = 1
CELLS = 16384
N_GZ = 8
N_GY = 4


def draw_positions(key, part):
    keys = jax.random.split(key, N_GZ * N_GY)
    orders = jax.vmap(lambda single: jax.random.permutation(single, BY * BX))(keys)
    return orders[:, :SLOTS].reshape(N_GZ, N_GY, SLOTS).astype(jnp.int32)


def draw_counts(key, part):
    base = jax.random.randint(jax.random.fold_in(key, 3), (N_GZ * N_GY,), 0, SLOTS)
    number = 1 + base * (base + 1) // SLOTS
    chosen = jax.random.randint(jax.random.fold_in(key, 7), (), 0, N_GZ * N_GY)
    number = jnp.where(jnp.arange(N_GZ * N_GY) == chosen, SLOTS, number)
    return number.reshape(N_GZ, N_GY).astype(jnp.int32)


def block_scale(own_key, extent, cuts, least, top_value):
    gain, own = 1.0, jax.random.fold_in(own_key, 6)
    for axis_at, blocks in cuts:
        steps = jnp.exp(jax.random.uniform(jax.random.fold_in(own, axis_at), (blocks,), jnp.float32, least / len(cuts), top_value / len(cuts)))
        gain = gain * jnp.repeat(steps, extent[axis_at] // blocks).reshape([-1 if axis == axis_at else 1 for axis in range(len(extent))])
    return gain


def scatter_about(stream_key, dims, deviation, most, shards=(), held_as=jnp.bfloat16):
    array = deviation * jax.random.normal(stream_key, dims, jnp.float32)
    if shards:
        array = array * block_scale(stream_key, dims, shards, -0.22, 0.18)
    return jnp.clip(array, -most, most).astype(held_as)


def setup_inputs(seed: int = 0) -> dict:
    streams_of = jax.random.split(jax.random.key(seed), 7)
    return {
        "features": scatter_about(streams_of[0], (N_GZ, N_GY, SLOTS, C, E ** 3), 1.0, 6.0, ((0, 8), (1, 4))),
        "cotangent": scatter_about(streams_of[1], (N_GZ, N_GY, SLOTS, C, E ** 3), 1.0, 6.0, ((0, 8), (1, 4))),
        "first_weight": scatter_about(streams_of[2], (C, 27 * C), (27 * C) ** -0.5, 0.15625),
        "second_weight": scatter_about(streams_of[3], (C, 27 * C), (27 * C) ** -0.5, 0.15625),
        "positions": draw_positions(jax.random.fold_in(streams_of[6], 71), 0),
        "counts": draw_counts(jax.random.fold_in(streams_of[6], 71), 0),
    }


def silu_slope(value):
    sig = jax.nn.sigmoid(value)
    return sig * (1.0 + value * (1.0 - sig))

def to_slab(bricks, places, live):
    channels = bricks.shape[1]
    masked = jnp.where(live[:, None, None], bricks, jnp.zeros_like(bricks))
    grid = jnp.zeros((BY * BX, channels, E ** 3), bricks.dtype).at[places].set(masked)
    grid = grid.reshape(BY, BX, channels, E, E, E)
    return grid.transpose(2, 3, 0, 4, 1, 5).reshape(channels, E, BY * E, BX * E)

def patch_of(padded, place):
    channels = padded.shape[0]
    zero = jnp.zeros((), jnp.int32)
    row_y = (place // BX).astype(jnp.int32) * E
    row_x = (place % BX).astype(jnp.int32) * E
    cube = lax.dynamic_slice(padded, (zero, zero, row_y, row_x), (channels, E + 2, E + 2, E + 2))
    pieces = []
    for depth in range(3):
        for height in range(3):
            for across in range(3):
                pieces.append(cube[:, depth:depth + E, height:height + E, across:across + E].reshape(channels, E ** 3))
    return jnp.concatenate(pieces, axis=0)

def flip_weight(weight):
    channels = weight.shape[0]
    return weight.reshape(channels, 27, channels)[:, ::-1, :].transpose(2, 1, 0).reshape(channels, 27 * channels)

def convolve(padded, weight, places):

    def single(place):
        return jnp.dot(weight, patch_of(padded, place), preferred_element_type=jnp.float32)
    return lax.map(single, places)

def weight_terms(padded, grads, places):
    channels = grads.shape[1]

    def step(total, item):
        place, grad_here = item
        term = lax.dot_general(grad_here, patch_of(padded, place), (((1,), (1,)), ((), ())), preferred_element_type=jnp.float32)
        return (total + term, 0)
    total, unused = lax.scan(step, jnp.zeros((channels, 27 * channels), jnp.float32), (places, grads))
    return total

def reference(features, cotangent, first_weight, second_weight, positions, counts):
    live_all = lax.iota(jnp.int32, SLOTS)[None, None, :] < counts[:, :, None]
    scale = 1.0 / math.sqrt(CELLS)

    def padded_of(all_bricks, iz, iy):
        rows = []
        for dz in (-1, 0, 1):
            row = []
            for dy in (-1, 0, 1):
                jz = iz + dz
                jy = iy + dy
                inside = (jz >= 0) & (jz < N_GZ) & (jy >= 0) & (jy < N_GY)
                cz = jnp.clip(jz, 0, N_GZ - 1)
                cy = jnp.clip(jy, 0, N_GY - 1)
                slab = to_slab(all_bricks[cz, cy], positions[cz, cy], live_all[cz, cy])
                row.append(jnp.where(inside, slab, jnp.zeros_like(slab)))
            rows.append(jnp.concatenate(row, axis=2))
        big = jnp.concatenate(rows, axis=1)
        cut = big[:, E - 1:2 * E + 1, BY * E - 1:2 * BY * E + 1, :]
        return jnp.pad(cut, ((0, 0), (0, 0), (0, 0), (1, 1)))

    def over_devices(fn):
        index = jnp.arange(N_GZ * N_GY, dtype=jnp.int32)
        result = lax.map(lambda d: fn(d // N_GY, d % N_GY), index)
        return jax.tree.map(lambda a: a.reshape((N_GZ, N_GY) + a.shape[1:]), result)

    def first_pass(iz, iy):
        live_col = live_all[iz, iy][:, None, None]
        pre = jnp.where(live_col, convolve(padded_of(features, iz, iy), first_weight, positions[iz, iy]), 0.0)
        return (pre, jax.nn.silu(pre).astype(jnp.bfloat16))
    first_pre, first_act = over_devices(first_pass)

    def second_pass(iz, iy):
        live_col = live_all[iz, iy][:, None, None]
        summed = features[iz, iy].astype(jnp.float32) + convolve(padded_of(first_act, iz, iy), second_weight, positions[iz, iy])
        result = jnp.where(live_col, jax.nn.silu(summed), 0.0).astype(jnp.bfloat16)
        grad_here = jnp.where(live_col, cotangent[iz, iy].astype(jnp.float32) * silu_slope(summed), 0.0).astype(jnp.bfloat16)
        return (result, grad_here)
    output, grad_sum = over_devices(second_pass)
    second_flip = flip_weight(second_weight)
    first_flip = flip_weight(first_weight)

    def third_pass(iz, iy):
        live_col = live_all[iz, iy][:, None, None]
        spread = convolve(padded_of(grad_sum, iz, iy), second_flip, positions[iz, iy])
        total = weight_terms(padded_of(first_act, iz, iy), grad_sum[iz, iy], positions[iz, iy])
        pre_grad = jnp.where(live_col, spread * silu_slope(first_pre[iz, iy]), 0.0).astype(jnp.bfloat16)
        return (pre_grad, total)
    pre_grad, second_terms = over_devices(third_pass)

    def fourth_pass(iz, iy):
        live_col = live_all[iz, iy][:, None, None]
        spread = convolve(padded_of(pre_grad, iz, iy), first_flip, positions[iz, iy])
        total = weight_terms(padded_of(features, iz, iy), pre_grad[iz, iy], positions[iz, iy])
        grad_in = jnp.where(live_col, grad_sum[iz, iy].astype(jnp.float32) + spread, 0.0).astype(jnp.bfloat16)
        return (grad_in, total)
    input_grad, first_terms = over_devices(fourth_pass)
    first_grad = lax.optimization_barrier(jnp.sum(first_terms, axis=(0, 1))) * scale
    second_grad = lax.optimization_barrier(jnp.sum(second_terms, axis=(0, 1))) * scale
    return (output, input_grad, first_grad, second_grad)
```

```python
import functools
import math

import jax
import jax.numpy as jnp
from jax import lax
from jax.experimental import pallas as pl
from jax.experimental.pallas import tpu as pltpu
from jax.sharding import PartitionSpec as P

E = 8
VOX = E**3
CH = 64
BX = 2
MESH = pl.DeviceIdType.MESH
F32 = jnp.float32
BF16 = jnp.bfloat16
FACES = ((-1, 0), (1, 0), (0, -1), (0, 1))
EDGES = ((-1, -1), (-1, 1), (1, -1), (1, 1))
PAIR = 2
TILES = 7
ROWS = 192
UNITS = ((0, 0, 896), (1, 0, 512), (1, 512, 896))


def sigmoid(value):
    return 1.0 / (1.0 + jnp.exp(-value))


def kernel(
    n_gz, n_gy,
    place_ref, count_ref, x_hbm, ct_hbm, w1_hbm, w2_hbm,
    out_ref, gin_ref, g1_ref, g2_ref,
    x_ref, ct_ref, w1_ref, w2_ref, in_sems,
    qx, qxo, qa, qao, qg, qp, pre, pre_o, sums, sums_o, xh, cth, acc,
    wt1, wt2, wf1, wf2, pre_s, gs_s, masks, masks_o, same, first,
    bf_send, bf_recv, be_send, be_recv, hf_send, hf_recv, he_send, he_recv,
    t_send, c_recv, t_sum, t_recv, z_recv, gath,
    c_ss, c_rs, f_ss, f_rs, bf_ss, bf_rs, be_ss, be_rs, hf_ss, hf_rs, he_ss, he_rs, t_ss, t_rs, z_ss, z_rs, g_ss, g_rs,
):
    gz = lax.axis_index("gz")
    gy = lax.axis_index("gy")
    members = PAIR * n_gy
    groups = n_gz // PAIR
    columns = n_gy // 2
    half = members // 2
    core = gy % 2
    mine = (gz % PAIR) * columns + gy // 2
    group = gz // PAIR

    def exists(dz, dy):
        ok = None
        for pos, step, count in ((gz, dz, n_gz), (gy, dy, n_gy)):
            if step:
                here = pos + step >= 0 if step < 0 else pos + step < count
                ok = here if ok is None else jnp.logical_and(ok, here)
        return ok

    def member_id(index):
        return (group * PAIR + index // columns, (index % columns) * 2 + core)

    sibling = (gz, gy + 1 - 2 * core)

    def group_id(index):
        return (index * PAIR + gz % PAIR, gy)

    for landing in (bf_recv, be_recv, hf_recv, he_recv):
        landing[...] = jnp.zeros_like(landing)
    barrier = pltpu.get_barrier_semaphore()
    total = jnp.int32(half + groups - 1)
    for dz, dy in FACES + EDGES:
        ok = exists(dz, dy)
        total = total + ok.astype(jnp.int32)

        @pl.when(ok)
        def _(dz=dz, dy=dy):
            pl.semaphore_signal(barrier, inc=1, device_id=(gz + dz, gy + dy), device_id_type=MESH)

    pl.semaphore_signal(barrier, inc=1, device_id=sibling, device_id_type=MESH)
    for r in range(1, half):
        pl.semaphore_signal(barrier, inc=1, device_id=member_id((mine + r) % half), device_id_type=MESH)
    for r in range(1, groups):
        pl.semaphore_signal(barrier, inc=1, device_id=group_id((group + r) % groups), device_id_type=MESH)

    loads = [
        pltpu.make_async_copy(src, dst, in_sems.at[n])
        for n, (src, dst) in enumerate(
            ((x_hbm, x_ref), (ct_hbm, ct_ref), (w1_hbm, w1_ref), (w2_hbm, w2_ref))
        )
    ]
    for load in loads:
        load.start()

    place = jnp.full((E, 128), place_ref[0], jnp.int32).astype(F32)
    live = jnp.full((E, 128), count_ref[0], jnp.int32).astype(F32)
    live = jnp.where(live > 0.5, 1.0, 0.0)
    lane = lax.broadcasted_iota(jnp.int32, (E, 128), 1)
    row = lax.broadcasted_iota(jnp.int32, (E, 128), 0)
    low = lane < CH
    code = (place + 1.0) * live

    def dup_t(block):
        return jnp.concatenate([block, block], axis=0).T

    def alive(value):
        return (value.reshape(-1, E, 128) * live[None]).reshape(value.shape)

    def x3(value):
        left = pltpu.roll(value, 1, 1)
        right = pltpu.roll(value, E - 1, 1)
        first = jnp.where(low[None], left, value)
        return jnp.concatenate([first, right], axis=-1)

    def halo_copy(e, kind, index):
        offsets, sends, recvs, ss, rs = (
            ((FACES, bf_send, bf_recv, bf_ss, bf_rs), (EDGES, be_send, be_recv, be_ss, be_rs)),
            ((FACES, hf_send, hf_recv, hf_ss, hf_rs), (EDGES, he_send, he_recv, he_ss, he_rs)),
        )[e][kind]
        dz, dy = offsets[index]
        slot = offsets.index((-dz, -dy))
        return pltpu.make_async_remote_copy(
            src_ref=sends.at[index],
            dst_ref=recvs.at[slot],
            send_sem=ss.at[index],
            recv_sem=rs.at[slot],
            device_id=(gz + dz, gy + dy),
            device_id_type=MESH,
        )

    def halo_start(e):
        for kind, offsets in ((1, EDGES), (0, FACES)):
            for index, (dz, dy) in enumerate(offsets):

                @pl.when(exists(dz, dy))
                def _(kind=kind, index=index):
                    halo_copy(e, kind, index).start()

    def near(step):
        return (0, 1, 2) if step < 0 else (E - 3, E - 2, E - 1)

    def rim(step):
        return 0 if step < 0 else E - 1

    def pack(one, two):
        return jnp.where(low, one, two).astype(BF16)

    def unpack(packed):
        value = packed.astype(F32)
        turned = pltpu.roll(value, CH, value.ndim - 1)
        return jnp.where(low, value, turned), jnp.where(low, turned, value)

    def bricks_pack(x, ct):
        x = x.reshape(E, E, E, 128)
        ct = ct.reshape(E, E, E, 128)
        for index, (dz, dy) in enumerate(FACES):
            layers = [x[n] if dz else x[:, n] for n in near(dz + dy)]
            layers.append(ct[rim(dz)] if dz else ct[:, rim(dy)])
            for n in range(2):
                bf_send[index, 64 * n : 64 * n + 64, :] = pack(layers[2 * n], layers[2 * n + 1]).reshape(64, 128)
            bf_send[index, 128:144, :] = jnp.concatenate([code, code], axis=0).astype(BF16)
        for index, (dz, dy) in enumerate(EDGES):
            lines = [x[m, n] for m in near(dz) for n in near(dy)] + [ct[rim(dz), rim(dy)]]
            packed = [jnp.where(low, lines[2 * n], lines[2 * n + 1]) for n in range(5)] + [code]
            be_send[index] = jnp.concatenate(packed, axis=0).astype(BF16)

    def thin_pack(value):
        cube = value.reshape(E, E, E, 128)
        for index, (dz, dy) in enumerate(FACES):
            face = cube[rim(dz)] if dz else cube[:, rim(dy)]
            hf_send[index] = face.reshape(64, 128).astype(BF16)
        for index, (dz, dy) in enumerate(EDGES):
            edge = cube[rim(dz), rim(dy)]
            he_send[index] = jnp.concatenate([edge, edge], axis=0).astype(BF16)

    def arrive(e, kind, indices):
        offsets = (FACES, EDGES)[kind]
        for index in indices:
            dz, dy = offsets[index]

            @pl.when(exists(dz, dy))
            def _(dz=dz, dy=dy):
                halo_copy(e, kind, offsets.index((-dz, -dy))).wait_recv()

    def sends_done(e):
        for kind, offsets in ((0, FACES), (1, EDGES)):
            for index, (dz, dy) in enumerate(offsets):

                @pl.when(exists(dz, dy))
                def _(kind=kind, index=index):
                    halo_copy(e, kind, index).wait_send()

    target0 = jnp.where(jnp.logical_and(low, row == 0), -1.0, 0.0)
    target1 = jnp.where(low, jnp.where(row == E - 1, 1.0, 0.0), 99.0)

    def x_mask(delta):
        return jnp.concatenate(
            [jnp.where(delta == target0, 1.0, 0.0), jnp.where(delta == target1, 1.0, 0.0)], axis=-1
        )

    own_y = jnp.where(place >= 1.5, 1.0, 0.0)
    own_x = place - 2.0 * own_y
    own_mask = x_mask(jnp.zeros((E, 128), F32))
    own_mask_o = x_mask(2.0 * own_x - 1.0)

    def wide(mask):
        return jnp.concatenate([mask, mask], axis=-1)

    def found(theirs):
        here = jnp.where(theirs > 0.5, 1.0, 0.0)
        their_y = jnp.where(theirs >= 2.5, 1.0, 0.0)
        their_x = theirs - 1.0 - 2.0 * their_y
        return here, their_y - own_y, their_x

    def make_masks():
        def put(block, parts):
            sides = [0.0, 0.0]
            alike = 0.0
            for keep, their_x in parts:
                sides[0] = sides[0] + wide(keep) * x_mask(their_x - own_x)
                sides[1] = sides[1] + wide(keep) * x_mask(their_x - 1.0 + own_x)
                alike = alike + keep * jnp.where(their_x == own_x, 1.0, 0.0)
            masks[block] = sides[0]
            masks_o[block] = sides[1]
            same[block] = alike

        for t in range(2):
            step = 2.0 * t - 1.0
            here, by, their_x = found(bf_recv[2 + t, 128:144, :].astype(F32)[0:E])
            put(6 + t, [(here * jnp.where(2.0 * step + by == step, 1.0, 0.0), their_x)])
        for s in range(2):
            here, by, their_x = found(bf_recv[s, 128:144, :].astype(F32)[0:E])
            put(3 * s + 1, [(here * jnp.where(by == 0.0, 1.0, 0.0), their_x)])
            for t in range(2):
                step = 2.0 * t - 1.0
                keep = here * jnp.where(by == step, 1.0, 0.0)
                here_e, by_e, their_xe = found(be_recv[2 * s + t, 32:48, :].astype(F32)[E : 2 * E])
                keep_e = here_e * jnp.where(2.0 * step + by_e == step, 1.0, 0.0)
                put(3 * s + 2 * t, [(keep, their_x), (keep_e, their_xe)])
                first[2 * s + t] = keep

    def span(n, depth):
        return ((0, depth), (depth, depth + E), (depth + E, 2 * depth + E))[n]

    def blocks(depth):
        for s in range(2):
            for n in range(3):
                yield 3 * s + n, span(2 * s, depth), span(n, depth)
        for t in range(2):
            yield 6 + t, span(1, depth), span(2 * t, depth)

    def fill(q, q_o, block, zs, ys, value):
        shape = (zs[1] - zs[0], ys[1] - ys[0], E, 256)
        spread = x3(value.reshape(-1, E, 128))
        mask = own_mask if block is None else masks[block]
        q[zs[0] : zs[1], ys[0] : ys[1]] = (spread * mask[None]).reshape(shape)
        if q_o is not None:
            mask = own_mask_o if block is None else masks_o[block]
            q_o[zs[0] : zs[1], ys[0] : ys[1]] = (spread * mask[None]).reshape(shape)

    def fill_own(q, q_o, depth, value):
        fill(q, q_o, None, span(1, depth), span(1, depth), value)

    def halo_bricks():
        faces = []
        for index in range(4):
            packed = bf_recv[index, 0:128, :].reshape(2, E, E, 128)
            one, two = unpack(packed[0])
            three, ct = unpack(packed[1])
            faces.append(([one, two, three], ct))
        for t in range(2):
            layers, ct = faces[2 + t]
            at = span(2 * t, 3)[0]
            for n, layer in enumerate(layers):
                fill(qx, qxo, 6 + t, (3, 3 + E), (at + n, at + n + 1), layer.reshape(E, 1, E, 128))
            y = t * (E + 1)
            xh[1 : E + 1, y] = layers[2 if t == 0 else 0]
            cth[1 : E + 1, y] = ct
        for s in range(2):
            layers, ct = faces[s]
            at = span(2 * s, 3)[0]
            edges = []
            for t in range(2):
                one, two = unpack(be_recv[2 * s + t, 0:48, :].reshape(6, E, 128)[0:5])
                edges.append([v for n in range(5) for v in (one[n], two[n])])
            z = s * (E + 1)
            for n, layer in enumerate(layers):
                fill(qx, qxo, 3 * s + 1, (at + n, at + n + 1), (3, 3 + E), layer[None])
                for t in range(2):
                    rows = layer[near(1 - 2 * t)[0] : near(1 - 2 * t)[0] + 3]
                    edge = jnp.stack(edges[t][3 * n : 3 * n + 3])
                    corner = jnp.where((first[2 * s + t] > 0.5)[None], rows, edge)
                    y0 = span(2 * t, 3)[0]
                    fill(qx, qxo, 3 * s + 2 * t, (at + n, at + n + 1), (y0, y0 + 3), corner[None])
                    if n == (2 if s == 0 else 0):
                        xh[z, t * (E + 1)] = corner[2 if t == 0 else 0]
            xh[z, 1 : E + 1] = layers[2 if s == 0 else 0]
            cth[z, 1 : E + 1] = ct
            for t in range(2):
                cth[z, t * (E + 1)] = jnp.where(first[2 * s + t] > 0.5, ct[rim(1 - 2 * t)], edges[t][9])

    def conv(w, rects):
        groups, count = [[]], 0
        for q, out, z0, z1, y0, y1 in rects:
            for z in range(z0, z1):
                size = (y1 - y0) * E
                if count + size > ROWS:
                    groups.append([])
                    count = 0
                groups[-1].append((q, out, z, y0, y1))
                count += size
        for group in groups:
            total = None
            for k in range(9):
                dz, dy = k // 3, k % 3
                rows = jnp.concatenate([q[z + dz, y0 + dy : y1 + dy].reshape(-1, 256) for q, out, z, y0, y1 in group], axis=0)
                part = jnp.dot(rows.astype(BF16), rows_of(w, k), preferred_element_type=F32)
                total = part if total is None else total + part
            at = 0
            for q, out, z, y0, y1 in group:
                size = (y1 - y0) * E
                out[z, y0:y1] = total[at : at + size].reshape(y1 - y0, E, 128)
                at += size

    def chosen(block, zs, ys, here, other):
        z0, z1 = zs
        y0, y1 = ys
        return jnp.where((same[block] > 0.5)[None, None], here[z0:z1, y0:y1], other[z0:z1, y0:y1])

    def patch(q, k, skip=0):
        dz, dy = k // 3 + skip, k % 3 + skip
        return q[dz : dz + E, dy : dy + E].reshape(VOX, 256).astype(BF16)

    def clear_halo(q):
        for plane in (0, E + 1):
            q[plane] = jnp.zeros((E + 2, E, 256), F32)
            q[1 : E + 1, plane] = jnp.zeros((E, E, 256), F32)

    def rows_of(w, k):
        return w[192 * k : 192 * k + 256, :]

    def conv_thin(q, w):
        def side(pieces):
            total = None
            for piece, k in pieces:
                part = jnp.dot(piece.reshape(64, 256).astype(BF16), rows_of(w, k), preferred_element_type=F32)
                total = part if total is None else total + part
            return total.reshape(E, E, 128)

        arrive(1, 0, (2, 3))
        for t in range(2):
            spread = x3(hf_recv[2 + t].astype(F32).reshape(E, E, 128))
            q[1 : E + 1, t * (E + 1)] = spread * masks[6 + t][None]
            acc[:, t * (E - 1)] += side(
                [(q[dz : dz + E, t * (E + 1)], 3 * dz + 2 * t) for dz in range(3)]
            )
        arrive(1, 1, range(4))
        arrive(1, 0, (0, 1))
        for s in range(2):
            plane = s * (E + 1)
            face = hf_recv[s].astype(F32).reshape(E, E, 128)
            q[plane, 1 : E + 1] = x3(face) * masks[3 * s + 1][None]
            for t in range(2):
                edge = he_recv[2 * s + t].astype(F32)[0:E]
                corner = jnp.where(first[2 * s + t] > 0.5, face[rim(1 - 2 * t)], edge)
                q[plane, t * (E + 1)] = x3(corner[None])[0] * masks[3 * s + 2 * t]
            acc[s * (E - 1)] += side([(q[plane, dy : dy + E], 6 * s + dy) for dy in range(3)])
        return acc[...].reshape(VOX, 128)

    def turn_weight(w_ref, wt):
        for t in range(13):
            wt[128 * t : 128 * t + 128, :] = dup_t(w_ref[:, 128 * t : 128 * t + 128].astype(F32)).astype(BF16)
        wt[1664:1728, :] = dup_t(w_ref[:, 1664:1728].astype(F32)).astype(BF16)
        wt[1728:1792, :] = jnp.zeros((64, 128), BF16)

    def flip_weight(w_ref, wf):
        low64 = lax.broadcasted_iota(jnp.int32, (64, 128), 1) < CH
        for t in range(13):
            tile = w_ref[:, 128 * t : 128 * t + 128].astype(F32)
            turned = pltpu.roll(tile, 64, 1)
            at = (26 - 2 * t) * 64
            wf[at : at + 64, :] = jnp.where(low64, tile, turned).astype(BF16)
            wf[at - 64 : at, :] = jnp.where(low64, turned, tile).astype(BF16)
        last = w_ref[:, 1664:1728].astype(F32)
        wf[0:64, :] = jnp.concatenate([last, last], axis=1).astype(BF16)
        wf[1728:1792, :] = jnp.zeros((64, 128), BF16)

    def terms(g, grads, q, skip, ready):
        turned = grads.T[0:CH].astype(BF16)

        def put(t, tile):
            for r in range(4):
                t_send[g, 2 * r + t % 2, :, 128 * (t // 2) : 128 * (t // 2) + 128] = tile[
                    16 * r : 16 * r + 16
                ].astype(BF16)

        for m in range(5):
            even = jnp.dot(turned, patch(q, 2 * m, skip), preferred_element_type=F32)
            put(3 * m, even[:, 0:128])
            if m == 4:
                put(3 * m + 1, even[:, 128:256])
            else:
                odd = jnp.dot(turned, patch(q, 2 * m + 1, skip), preferred_element_type=F32)
                odd = pltpu.roll(odd, 64, 1)
                put(3 * m + 1, even[:, 128:256] + odd[:, 0:128])
                put(3 * m + 2, odd[:, 128:256])
            if m in ready:
                pair_copy(ready[m]).start()

    def part_of(buffer, u, slot):
        g, lo, hi = UNITS[u]
        return buffer.at[g, slot, :, lo:hi]

    def half_of(buffer, u, side):
        g, lo, hi = UNITS[u]
        return buffer.at[g, pl.ds(side * half, half), :, lo:hi]

    def pair_copy(u):
        return pltpu.make_async_remote_copy(
            src_ref=half_of(t_send, u, 1 - core), dst_ref=half_of(c_recv, u, 0),
            send_sem=c_ss.at[u], recv_sem=c_rs.at[u], device_id=sibling, device_id_type=MESH,
        )

    def t_copy(u, r):
        to = (mine + r) % half
        return pltpu.make_async_remote_copy(
            src_ref=part_of(t_sum, u, to), dst_ref=part_of(t_recv, u, mine),
            send_sem=t_ss.at[u, r], recv_sem=t_rs.at[u, r],
            device_id=member_id(to), device_id_type=MESH,
        )

    def z_copy(u, r):
        return pltpu.make_async_remote_copy(
            src_ref=part_of(z_recv, u, group), dst_ref=part_of(z_recv, u, group),
            send_sem=z_ss.at[u, r], recv_sem=z_rs.at[u, r],
            device_id=group_id((group + r) % groups), device_id_type=MESH,
        )

    def g_copy(u, r):
        return pltpu.make_async_remote_copy(
            src_ref=part_of(gath, u, core * half + mine), dst_ref=part_of(gath, u, core * half + mine),
            send_sem=g_ss.at[u, r], recv_sem=g_rs.at[u, r],
            device_id=member_id((mine + r) % half), device_id_type=MESH,
        )

    def f_copy(u, side):
        return pltpu.make_async_remote_copy(
            src_ref=half_of(gath, u, side), dst_ref=half_of(gath, u, side),
            send_sem=f_ss.at[u], recv_sem=f_rs.at[u], device_id=sibling, device_id_type=MESH,
        )

    def recv_of(buffer, u, slot, ss, rs, r):
        return pltpu.make_async_remote_copy(
            src_ref=part_of(buffer, u, slot), dst_ref=part_of(buffer, u, slot),
            send_sem=ss.at[u, r], recv_sem=rs.at[u, r],
            device_id=member_id((mine + 1) % half), device_id_type=MESH,
        )

    def add_up(buffer, u, count):
        g, lo, hi = UNITS[u]
        total = buffer[g, 0, :, lo:hi].astype(F32)
        for n in range(1, count):
            total = total + buffer[g, n, :, lo:hi].astype(F32)
        return total.astype(BF16)

    def scatter_start(u):
        g, lo, hi = UNITS[u]
        pair_copy(u).wait_recv()
        own = t_send[g, pl.ds(core * half, half), :, lo:hi].astype(F32)
        t_sum[g, :, :, lo:hi] = (own + c_recv[g, :, :, lo:hi].astype(F32)).astype(BF16)
        for r in range(1, half):
            t_copy(u, r).start()
        t_recv[g, mine, :, lo:hi] = t_sum[g, mine, :, lo:hi]

    def exchange_start(u):
        g, lo, hi = UNITS[u]
        for r in range(1, half):
            recv_of(t_recv, u, (mine + half - r) % half, t_ss, t_rs, r).wait_recv()
        z_recv[g, group, :, lo:hi] = add_up(t_recv, u, half)
        for r in range(1, groups):
            z_copy(u, r).start()

    def gather_start(u):
        g, lo, hi = UNITS[u]
        for r in range(1, groups):
            recv_of(z_recv, u, (group + groups - r) % groups, z_ss, z_rs, r).wait_recv()
        gath[g, core * half + mine, :, lo:hi] = add_up(z_recv, u, groups)
        for r in range(1, half):
            g_copy(u, r).start()

    def forward_start(u):
        for r in range(1, half):
            recv_of(gath, u, core * half + (mine + half - r) % half, g_ss, g_rs, r).wait_recv()
        f_copy(u, core).start()

    def gather_end(u, ref):
        g, lo, hi = UNITS[u]
        f_copy(u, 1 - core).wait_recv()
        for r in range(4):
            for t in range(2 * lo // 128, 2 * hi // 128):
                end = min(128 * t + 128, 27 * CH)
                at = 128 * (t // 2)
                ref[16 * r : 16 * r + 16, 128 * t : end] = gath[
                    g, 2 * r + t % 2, :, at : at + end - 128 * t
                ]

    def reduce_done(u):
        pair_copy(u).wait_send()
        f_copy(u, core).wait_send()
        for r in range(1, half):
            t_copy(u, r).wait_send()
            g_copy(u, r).wait_send()
        for r in range(1, groups):
            z_copy(u, r).wait_send()

    clear_halo(qp)
    loads[0].wait()
    x = dup_t(x_ref[...].astype(F32))
    field = alive(x)
    loads[1].wait()
    ct = alive(dup_t(ct_ref[...].astype(F32)))
    bricks_pack(field, ct)
    pl.semaphore_wait(barrier, total)
    halo_start(0)
    fill_own(qx, qxo, 3, field)
    xh[1 : E + 1, 1 : E + 1] = x.reshape(E, E, E, 128)
    cth[1 : E + 1, 1 : E + 1] = ct.reshape(E, E, E, 128)
    loads[2].wait()
    turn_weight(w1_ref, wt1)
    conv(wt1, [(qx, pre, 3, 9, 3, 9)])
    loads[3].wait()
    turn_weight(w2_ref, wt2)
    flip_weight(w2_ref, wf2)
    flip_weight(w1_ref, wf1)
    arrive(0, 0, range(4))
    arrive(0, 1, range(4))
    make_masks()
    halo_bricks()
    conv(
        wt1,
        [
            (qx, pre, 0, 3, 0, 12), (qx, pre, 9, 12, 0, 12), (qx, pre, 3, 9, 0, 3), (qx, pre, 3, 9, 9, 12),
            (qxo, pre_o, 0, 2, 0, 12), (qxo, pre_o, 10, 12, 0, 12),
            (qxo, pre_o, 2, 10, 0, 2), (qxo, pre_o, 2, 10, 10, 12),
        ],
    )

    def silu(value):
        return (value * sigmoid(value)).astype(BF16).astype(F32)

    own = pre[2:10, 2:10].reshape(VOX, 128)
    act = alive(silu(own))
    fill_own(qa, qao, 2, act)
    for block, zs, ys in blocks(2):
        fill(qa, qao, block, zs, ys, silu(chosen(block, zs, ys, pre, pre_o)))
    conv(
        wt2,
        [
            (qa, sums, 0, 10, 0, 10),
            (qao, sums_o, 0, 1, 0, 10), (qao, sums_o, 9, 10, 0, 10),
            (qao, sums_o, 1, 9, 0, 1), (qao, sums_o, 1, 9, 9, 10),
        ],
    )

    def slope(value):
        sig = sigmoid(value)
        return sig, sig * (1.0 + value * (1.0 - sig))

    summed = x + sums[1:9, 1:9].reshape(VOX, 128)
    sig, steep = slope(summed)
    gs = alive(ct * steep).astype(BF16).astype(F32)
    gs_s[...] = gs
    out_ref[...] = alive(summed * sig).T[0:CH].astype(BF16)
    fill_own(qg, None, 1, gs)
    for block, zs, ys in blocks(1):
        near_sum = chosen(block, zs, ys, sums, sums_o) + xh[zs[0] : zs[1], ys[0] : ys[1]]
        near_gs = cth[zs[0] : zs[1], ys[0] : ys[1]] * slope(near_sum)[1]
        fill(qg, None, block, zs, ys, near_gs.astype(BF16).astype(F32))
    pre_s[...] = slope(own)[1]
    terms(0, gs, qa, 1, {4: 0})
    conv(wf2, [(qg, acc, 0, E, 0, E)])
    pg = alive(acc[...].reshape(VOX, 128) * pre_s[...]).astype(BF16).astype(F32)

    scatter_start(0)
    terms(1, pg, qx, 2, {2: 1, 4: 2})
    thin_pack(pg)
    scatter_start(1)
    halo_start(1)
    scatter_start(2)
    fill_own(qp, None, 1, pg)
    exchange_start(0)
    conv(wf1, [(qp, acc, 0, E, 0, E)])
    exchange_start(1)
    exchange_start(2)
    gather_start(0)
    gin = alive(gs_s[...] + conv_thin(qp, wf1))
    gather_start(1)
    gather_start(2)
    forward_start(0)
    gin_ref[...] = gin.T[0:CH].astype(BF16)
    forward_start(1)
    forward_start(2)
    for e in range(2):
        sends_done(e)
    gather_end(0, g2_ref)
    gather_end(1, g1_ref)
    gather_end(2, g1_ref)
    for u in range(3):
        reduce_done(u)


def finish(scale, out_in, gin_in, g1_in, g2_in, out_ref, gin_ref, g1_ref, g2_ref):
    out_ref[...] = out_in[...]
    gin_ref[...] = gin_in[...]
    g1_ref[...] = g1_in[...].astype(F32) * scale
    g2_ref[...] = g2_in[...].astype(F32) * scale


def body(features, cotangent, first_weight, second_weight, positions, counts):
    n_gz = lax.axis_size("gz")
    n_gy = lax.axis_size("gy")
    slots = features.shape[2]
    scale = 1.0 / math.sqrt(n_gz * n_gy * slots * VOX)
    members = PAIR * n_gy
    groups = n_gz // PAIR
    vmem = pl.BlockSpec(memory_space=pltpu.VMEM)
    smem = pl.BlockSpec(memory_space=pltpu.SMEM)
    dma = pltpu.SemaphoreType.DMA
    hbm = pl.BlockSpec(memory_space=pl.ANY)
    output, input_grad, first_sum, second_sum = pl.pallas_call(
        functools.partial(kernel, n_gz, n_gy),
        out_shape=(
            pltpu.VMEM((CH, VOX), BF16),
            pltpu.VMEM((CH, VOX), BF16),
            pltpu.VMEM((CH, 27 * CH), BF16),
            pltpu.VMEM((CH, 27 * CH), BF16),
        ),
        in_specs=[smem, smem, hbm, hbm, hbm, hbm],
        out_specs=(vmem,) * 4,
        scratch_shapes=[
            pltpu.VMEM((CH, VOX), BF16),
            pltpu.VMEM((CH, VOX), BF16),
            pltpu.VMEM((CH, 27 * CH), BF16),
            pltpu.VMEM((CH, 27 * CH), BF16),
            dma((4,)),
            pltpu.VMEM((E + 6, E + 6, E, 256), F32),
            pltpu.VMEM((E + 6, E + 6, E, 256), F32),
            pltpu.VMEM((E + 4, E + 4, E, 256), F32),
            pltpu.VMEM((E + 4, E + 4, E, 256), F32),
            pltpu.VMEM((E + 2, E + 2, E, 256), F32),
            pltpu.VMEM((E + 2, E + 2, E, 256), F32),
            pltpu.VMEM((E + 4, E + 4, E, 128), F32),
            pltpu.VMEM((E + 4, E + 4, E, 128), F32),
            pltpu.VMEM((E + 2, E + 2, E, 128), F32),
            pltpu.VMEM((E + 2, E + 2, E, 128), F32),
            pltpu.VMEM((E + 2, E + 2, E, 128), F32),
            pltpu.VMEM((E + 2, E + 2, E, 128), F32),
            pltpu.VMEM((E, E, E, 128), F32),
            pltpu.VMEM((1792, 128), BF16),
            pltpu.VMEM((1792, 128), BF16),
            pltpu.VMEM((1792, 128), BF16),
            pltpu.VMEM((1792, 128), BF16),
            pltpu.VMEM((VOX, 128), F32),
            pltpu.VMEM((VOX, 128), F32),
            pltpu.VMEM((8, E, 256), F32),
            pltpu.VMEM((8, E, 256), F32),
            pltpu.VMEM((8, E, 128), F32),
            pltpu.VMEM((4, E, 128), F32),
            pltpu.VMEM((4, 144, 128), BF16),
            pltpu.VMEM((4, 144, 128), BF16),
            pltpu.VMEM((4, 48, 128), BF16),
            pltpu.VMEM((4, 48, 128), BF16),
            pltpu.VMEM((4, 64, 128), BF16),
            pltpu.VMEM((4, 64, 128), BF16),
            pltpu.VMEM((4, 16, 128), BF16),
            pltpu.VMEM((4, 16, 128), BF16),
            pltpu.VMEM((2, members, 16, 128 * TILES), BF16),
            pltpu.VMEM((2, members // 2, 16, 128 * TILES), BF16),
            pltpu.VMEM((2, members // 2, 16, 128 * TILES), BF16),
            pltpu.VMEM((2, members // 2, 16, 128 * TILES), BF16),
            pltpu.VMEM((2, groups, 16, 128 * TILES), BF16),
            pltpu.VMEM((2, members, 16, 128 * TILES), BF16),
            dma((3,)), dma((3,)), dma((3,)), dma((3,)),
            dma((4,)), dma((4,)), dma((4,)), dma((4,)), dma((4,)), dma((4,)), dma((4,)), dma((4,)),
            dma((3, members)), dma((3, members)),
            dma((3, groups)), dma((3, groups)),
            dma((3, members)), dma((3, members)),
        ],
        compiler_params=pltpu.CompilerParams(collective_id=0, has_side_effects=True),
    )(
        positions.reshape(1), counts.reshape(1), features[0, 0, 0], cotangent[0, 0, 0],
        first_weight, second_weight,
    )
    grad = jax.ShapeDtypeStruct((CH, 27 * CH), F32)
    brick = jax.ShapeDtypeStruct((CH, VOX), BF16)
    output, input_grad, first_grad, second_grad = pl.pallas_call(
        functools.partial(finish, scale),
        out_shape=(brick, brick, grad, grad),
        in_specs=[vmem] * 4,
        out_specs=(vmem,) * 4,
    )(*(
        pltpu.with_memory_space_constraint(value, pltpu.VMEM)
        for value in (output, input_grad, first_sum, second_sum)
    ))
    return (output[None, None, None], input_grad[None, None, None], first_grad, second_grad)


def solution(mesh):
    return jax.shard_map(
        body,
        mesh=mesh,
        in_specs=(
            P("gz", "gy", None, None, None),
            P("gz", "gy", None, None, None),
            P(),
            P(),
            P("gz", "gy", None),
            P("gz", "gy"),
        ),
        out_specs=(P("gz", "gy", None, None, None), P("gz", "gy", None, None, None), P(), P()),
        check_vma=False,
    )
```

```python
import functools
import math

import jax
import jax.numpy as jnp
from jax import lax
from jax.experimental import pallas as pl
from jax.experimental.pallas import tpu as pltpu
from jax.sharding import PartitionSpec as P

E = 8
VOX = E**3
CH = 64
BX = 2
MESH = pl.DeviceIdType.MESH
F32 = jnp.float32
BF16 = jnp.bfloat16
FACES = ((-1, 0), (1, 0), (0, -1), (0, 1))
EDGES = ((-1, -1), (-1, 1), (1, -1), (1, 1))
PAIR = 2
TILES = 7
ROWS = 256
UNITS = ((0, 0, 896), (1, 0, 512), (1, 512, 896))


def sigmoid(value):
    return 1.0 / (1.0 + jnp.exp(-value))


def kernel(
    n_gz, n_gy,
    place_ref, count_ref, x_hbm, ct_hbm, w1_hbm, w2_hbm,
    out_ref, gin_ref, g1_ref, g2_ref,
    x_ref, ct_ref, w1_ref, w2_ref, in_sems,
    qx, qxo, qa, qao, qg, qp, pre, pre_o, sums, sums_o, xh, cth, acc,
    wt1, wt2, wf1, wf2, wn1, wn2, wm1, wm2, pre_s, gs_s, masks, masks_o, same, first,
    bf_send, bf_recv, be_send, be_recv, hf_send, hf_recv, he_send, he_recv,
    t_send, c_recv, t_sum, t_recv, z_recv, gath,
    c_ss, c_rs, f_ss, f_rs, bf_ss, bf_rs, be_ss, be_rs, hf_ss, hf_rs, he_ss, he_rs, t_ss, t_rs, z_ss, z_rs, g_ss, g_rs,
):
    gz = lax.axis_index("gz")
    gy = lax.axis_index("gy")
    members = PAIR * n_gy
    groups = n_gz // PAIR
    columns = n_gy // 2
    half = members // 2
    core = gy % 2
    mine = (gz % PAIR) * columns + gy // 2
    group = gz // PAIR

    def exists(dz, dy):
        ok = None
        for pos, step, count in ((gz, dz, n_gz), (gy, dy, n_gy)):
            if step:
                here = pos + step >= 0 if step < 0 else pos + step < count
                ok = here if ok is None else jnp.logical_and(ok, here)
        return ok

    def member_id(index):
        return (group * PAIR + index // columns, (index % columns) * 2 + core)

    sibling = (gz, gy + 1 - 2 * core)

    def group_id(index):
        return (index * PAIR + gz % PAIR, gy)

    for landing in (bf_recv, be_recv, hf_recv, he_recv):
        landing[...] = jnp.zeros_like(landing)
    barrier = pltpu.get_barrier_semaphore()
    total = jnp.int32(half + groups - 1)
    for dz, dy in EDGES + FACES:
        ok = exists(dz, dy)
        total = total + ok.astype(jnp.int32)

        @pl.when(ok)
        def _(dz=dz, dy=dy):
            pl.semaphore_signal(barrier, inc=1, device_id=(gz + dz, gy + dy), device_id_type=MESH)

    pl.semaphore_signal(barrier, inc=1, device_id=sibling, device_id_type=MESH)
    for r in range(1, half):
        pl.semaphore_signal(barrier, inc=1, device_id=member_id((mine + r) % half), device_id_type=MESH)
    for r in range(1, groups):
        pl.semaphore_signal(barrier, inc=1, device_id=group_id((group + r) % groups), device_id_type=MESH)

    loads = [
        pltpu.make_async_copy(src, dst, in_sems.at[n])
        for n, (src, dst) in enumerate(
            ((x_hbm, x_ref), (ct_hbm, ct_ref), (w1_hbm, w1_ref), (w2_hbm, w2_ref))
        )
    ]
    for load in loads:
        load.start()

    place = jnp.full((E, 128), place_ref[0], jnp.int32).astype(F32)
    live = jnp.full((E, 128), count_ref[0], jnp.int32).astype(F32)
    live = jnp.where(live > 0.5, 1.0, 0.0)
    lane = lax.broadcasted_iota(jnp.int32, (E, 128), 1)
    row = lax.broadcasted_iota(jnp.int32, (E, 128), 0)
    low = lane < CH
    code = (place + 1.0) * live

    def dup_t(block):
        return jnp.concatenate([block, block], axis=0).T

    def alive(value):
        return (value.reshape(-1, E, 128) * live[None]).reshape(value.shape)

    def x3(value):
        left = pltpu.roll(value, 1, 1)
        right = pltpu.roll(value, E - 1, 1)
        first = jnp.where(low[None], left, value)
        return jnp.concatenate([first, right], axis=-1)

    def halo_copy(e, kind, index):
        offsets, sends, recvs, ss, rs = (
            ((FACES, bf_send, bf_recv, bf_ss, bf_rs), (EDGES, be_send, be_recv, be_ss, be_rs)),
            ((FACES, hf_send, hf_recv, hf_ss, hf_rs), (EDGES, he_send, he_recv, he_ss, he_rs)),
        )[e][kind]
        dz, dy = offsets[index]
        slot = offsets.index((-dz, -dy))
        return pltpu.make_async_remote_copy(
            src_ref=sends.at[index],
            dst_ref=recvs.at[slot],
            send_sem=ss.at[index],
            recv_sem=rs.at[slot],
            device_id=(gz + dz, gy + dy),
            device_id_type=MESH,
        )

    def halo_start(e):
        for kind, offsets in ((1, EDGES), (0, FACES)):
            for index, (dz, dy) in enumerate(offsets):

                @pl.when(exists(dz, dy))
                def _(kind=kind, index=index):
                    halo_copy(e, kind, index).start()

    def near(step):
        return (0, 1, 2) if step < 0 else (E - 3, E - 2, E - 1)

    def rim(step):
        return 0 if step < 0 else E - 1

    def pack(one, two):
        return jnp.where(low, one, two).astype(BF16)

    def unpack(packed):
        value = packed.astype(F32)
        turned = pltpu.roll(value, CH, value.ndim - 1)
        return jnp.where(low, value, turned), jnp.where(low, turned, value)

    def bricks_pack(x, ct):
        x = x.reshape(E, E, E, 128)
        ct = ct.reshape(E, E, E, 128)
        for index, (dz, dy) in enumerate(FACES):
            layers = [x[n] if dz else x[:, n] for n in near(dz + dy)]
            layers.append(ct[rim(dz)] if dz else ct[:, rim(dy)])
            for n in range(2):
                bf_send[index, 64 * n : 64 * n + 64, :] = pack(layers[2 * n], layers[2 * n + 1]).reshape(64, 128)
            bf_send[index, 128:144, :] = jnp.concatenate([code, code], axis=0).astype(BF16)
        for index, (dz, dy) in enumerate(EDGES):
            lines = [x[m, n] for m in near(dz) for n in near(dy)] + [ct[rim(dz), rim(dy)]]
            packed = [jnp.where(low, lines[2 * n], lines[2 * n + 1]) for n in range(5)] + [code]
            be_send[index] = jnp.concatenate(packed, axis=0).astype(BF16)

    def thin_pack(value):
        cube = value.reshape(E, E, E, 128)
        for index, (dz, dy) in enumerate(FACES):
            face = cube[rim(dz)] if dz else cube[:, rim(dy)]
            hf_send[index] = face.reshape(64, 128).astype(BF16)
        for index, (dz, dy) in enumerate(EDGES):
            edge = cube[rim(dz), rim(dy)]
            he_send[index] = jnp.concatenate([edge, edge], axis=0).astype(BF16)

    def arrive(e, kind, indices):
        offsets = (FACES, EDGES)[kind]
        for index in indices:
            dz, dy = offsets[index]

            @pl.when(exists(dz, dy))
            def _(dz=dz, dy=dy):
                halo_copy(e, kind, offsets.index((-dz, -dy))).wait_recv()

    def sends_done(e):
        for kind, offsets in ((0, FACES), (1, EDGES)):
            for index, (dz, dy) in enumerate(offsets):

                @pl.when(exists(dz, dy))
                def _(kind=kind, index=index):
                    halo_copy(e, kind, index).wait_send()

    target0 = jnp.where(jnp.logical_and(low, row == 0), -1.0, 0.0)
    target1 = jnp.where(low, jnp.where(row == E - 1, 1.0, 0.0), 99.0)

    def x_mask(delta):
        return jnp.concatenate(
            [jnp.where(delta == target0, 1.0, 0.0), jnp.where(delta == target1, 1.0, 0.0)], axis=-1
        )

    own_y = jnp.where(place >= 1.5, 1.0, 0.0)
    own_x = place - 2.0 * own_y
    own_mask = x_mask(jnp.zeros((E, 128), F32))
    own_mask_o = x_mask(2.0 * own_x - 1.0)

    def wide(mask):
        return jnp.concatenate([mask, mask], axis=-1)

    def found(theirs):
        here = jnp.where(theirs > 0.5, 1.0, 0.0)
        their_y = jnp.where(theirs >= 2.5, 1.0, 0.0)
        their_x = theirs - 1.0 - 2.0 * their_y
        return here, their_y - own_y, their_x

    def make_masks():
        def put(block, parts):
            sides = [0.0, 0.0]
            alike = 0.0
            for keep, their_x in parts:
                sides[0] = sides[0] + wide(keep) * x_mask(their_x - own_x)
                sides[1] = sides[1] + wide(keep) * x_mask(their_x - 1.0 + own_x)
                alike = alike + keep * jnp.where(their_x == own_x, 1.0, 0.0)
            masks[block] = sides[0]
            masks_o[block] = sides[1]
            same[block] = alike

        for t in range(2):
            step = 2.0 * t - 1.0
            here, by, their_x = found(bf_recv[2 + t, 128:144, :].astype(F32)[0:E])
            put(6 + t, [(here * jnp.where(2.0 * step + by == step, 1.0, 0.0), their_x)])
        for s in range(2):
            here, by, their_x = found(bf_recv[s, 128:144, :].astype(F32)[0:E])
            put(3 * s + 1, [(here * jnp.where(by == 0.0, 1.0, 0.0), their_x)])
            for t in range(2):
                step = 2.0 * t - 1.0
                keep = here * jnp.where(by == step, 1.0, 0.0)
                here_e, by_e, their_xe = found(be_recv[2 * s + t, 32:48, :].astype(F32)[E : 2 * E])
                keep_e = here_e * jnp.where(2.0 * step + by_e == step, 1.0, 0.0)
                put(3 * s + 2 * t, [(keep, their_x), (keep_e, their_xe)])
                first[2 * s + t] = keep

    def span(n, depth):
        return ((0, depth), (depth, depth + E), (depth + E, 2 * depth + E))[n]

    def blocks(depth):
        for s in range(2):
            for n in range(3):
                yield 3 * s + n, span(2 * s, depth), span(n, depth)
        for t in range(2):
            yield 6 + t, span(1, depth), span(2 * t, depth)

    def fill(q, q_o, block, zs, ys, value):
        shape = (zs[1] - zs[0], ys[1] - ys[0], E, 256)
        spread = x3(value.reshape(-1, E, 128))
        mask = own_mask if block is None else masks[block]
        q[zs[0] : zs[1], ys[0] : ys[1]] = (spread * mask[None]).reshape(shape)
        if q_o is not None:
            mask = own_mask_o if block is None else masks_o[block]
            q_o[zs[0] : zs[1], ys[0] : ys[1]] = (spread * mask[None]).reshape(shape)

    def fill_own(q, q_o, depth, value):
        fill(q, q_o, None, span(1, depth), span(1, depth), value)

    def halo_bricks():
        faces = []
        for index in range(4):
            packed = bf_recv[index, 0:128, :].reshape(2, E, E, 128)
            one, two = unpack(packed[0])
            three, ct = unpack(packed[1])
            faces.append(([one, two, three], ct))
        for t in range(2):
            layers, ct = faces[2 + t]
            at = span(2 * t, 3)[0]
            for n, layer in enumerate(layers):
                fill(qx, qxo, 6 + t, (3, 3 + E), (at + n, at + n + 1), layer.reshape(E, 1, E, 128))
            y = t * (E + 1)
            xh[1 : E + 1, y] = layers[2 if t == 0 else 0]
            cth[1 : E + 1, y] = ct
        for s in range(2):
            layers, ct = faces[s]
            at = span(2 * s, 3)[0]
            edges = []
            for t in range(2):
                one, two = unpack(be_recv[2 * s + t, 0:48, :].reshape(6, E, 128)[0:5])
                edges.append([v for n in range(5) for v in (one[n], two[n])])
            z = s * (E + 1)
            for n, layer in enumerate(layers):
                fill(qx, qxo, 3 * s + 1, (at + n, at + n + 1), (3, 3 + E), layer[None])
                for t in range(2):
                    rows = layer[near(1 - 2 * t)[0] : near(1 - 2 * t)[0] + 3]
                    edge = jnp.stack(edges[t][3 * n : 3 * n + 3])
                    corner = jnp.where((first[2 * s + t] > 0.5)[None], rows, edge)
                    y0 = span(2 * t, 3)[0]
                    fill(qx, qxo, 3 * s + 2 * t, (at + n, at + n + 1), (y0, y0 + 3), corner[None])
                    if n == (2 if s == 0 else 0):
                        xh[z, t * (E + 1)] = corner[2 if t == 0 else 0]
            xh[z, 1 : E + 1] = layers[2 if s == 0 else 0]
            cth[z, 1 : E + 1] = ct
            for t in range(2):
                cth[z, t * (E + 1)] = jnp.where(first[2 * s + t] > 0.5, ct[rim(1 - 2 * t)], edges[t][9])

    def merge_weight(w, wn):
        low256 = lax.broadcasted_iota(jnp.int32, (256, 128), 1) < CH
        for dy in range(3):
            outer = jnp.where(low256, rows_of(w, dy).astype(F32), rows_of(w, 6 + dy).astype(F32))
            wn[256 * dy : 256 * dy + 256, 0:128] = outer.astype(BF16)
            wn[256 * dy : 256 * dy + 256, 128:256] = rows_of(w, 3 + dy)

    def conv(wn, rects):
        groups, count = [[]], 0
        for q, out, z0, z1, y0, y1 in rects:
            for z in range(z0, z1 + 2):
                size = (y1 - y0) * E
                if count + size > ROWS:
                    groups.append([])
                    count = 0
                groups[-1].append((q, out, z, z0, y0, y1))
                count += size
        held = {}
        for group in groups:
            total = None
            for dy in range(3):
                rows = [q[z, y0 + dy : y1 + dy].reshape(-1, 256) for q, out, z, z0, y0, y1 in group]
                rows = jnp.concatenate(rows, axis=0).astype(BF16)
                part = jnp.dot(rows, wn[256 * dy : 256 * dy + 256, :], preferred_element_type=F32)
                total = part if total is None else total + part
            at = 0
            for q, out, z, z0, y0, y1 in group:
                size = (y1 - y0) * E
                outer = total[at : at + size, 0:128].reshape(y1 - y0, E, 128)
                inner = total[at : at + size, 128:256].reshape(y1 - y0, E, 128)
                at += size
                turned = pltpu.roll(outer, CH, 2)
                if z == z0:
                    held = {}
                held[z] = (jnp.where(low, outer, turned), inner, jnp.where(low, turned, outer))
                if z >= z0 + 2:
                    out[z - 2, y0:y1] = held[z - 2][0] + held[z - 1][1] + held[z][2]

    def chosen(block, zs, ys, here, other):
        z0, z1 = zs
        y0, y1 = ys
        return jnp.where((same[block] > 0.5)[None, None], here[z0:z1, y0:y1], other[z0:z1, y0:y1])

    def patch(q, k, skip=0):
        dz, dy = k // 3 + skip, k % 3 + skip
        return q[dz : dz + E, dy : dy + E].reshape(VOX, 256).astype(BF16)

    def clear_halo(q):
        for plane in (0, E + 1):
            q[plane] = jnp.zeros((E + 2, E, 256), F32)
            q[1 : E + 1, plane] = jnp.zeros((E, E, 256), F32)

    def rows_of(w, k):
        return w[192 * k : 192 * k + 256, :]

    def conv_thin(q, w):
        def side(pieces):
            total = None
            for piece, k in pieces:
                part = jnp.dot(piece.reshape(64, 256).astype(BF16), rows_of(w, k), preferred_element_type=F32)
                total = part if total is None else total + part
            return total.reshape(E, E, 128)

        arrive(1, 0, (2, 3))
        for t in range(2):
            spread = x3(hf_recv[2 + t].astype(F32).reshape(E, E, 128))
            q[1 : E + 1, t * (E + 1)] = spread * masks[6 + t][None]
            acc[:, t * (E - 1)] += side(
                [(q[dz : dz + E, t * (E + 1)], 3 * dz + 2 * t) for dz in range(3)]
            )
        arrive(1, 1, range(4))
        arrive(1, 0, (0, 1))
        for s in range(2):
            plane = s * (E + 1)
            face = hf_recv[s].astype(F32).reshape(E, E, 128)
            q[plane, 1 : E + 1] = x3(face) * masks[3 * s + 1][None]
            for t in range(2):
                edge = he_recv[2 * s + t].astype(F32)[0:E]
                corner = jnp.where(first[2 * s + t] > 0.5, face[rim(1 - 2 * t)], edge)
                q[plane, t * (E + 1)] = x3(corner[None])[0] * masks[3 * s + 2 * t]
            acc[s * (E - 1)] += side([(q[plane, dy : dy + E], 6 * s + dy) for dy in range(3)])
        return acc[...].reshape(VOX, 128)

    def turn_weight(w_ref, wt):
        for t in range(13):
            wt[128 * t : 128 * t + 128, :] = dup_t(w_ref[:, 128 * t : 128 * t + 128].astype(F32)).astype(BF16)
        wt[1664:1728, :] = dup_t(w_ref[:, 1664:1728].astype(F32)).astype(BF16)
        wt[1728:1792, :] = jnp.zeros((64, 128), BF16)

    def flip_weight(w_ref, wf):
        low64 = lax.broadcasted_iota(jnp.int32, (64, 128), 1) < CH
        for t in range(13):
            tile = w_ref[:, 128 * t : 128 * t + 128].astype(F32)
            turned = pltpu.roll(tile, 64, 1)
            at = (26 - 2 * t) * 64
            wf[at : at + 64, :] = jnp.where(low64, tile, turned).astype(BF16)
            wf[at - 64 : at, :] = jnp.where(low64, turned, tile).astype(BF16)
        last = w_ref[:, 1664:1728].astype(F32)
        wf[0:64, :] = jnp.concatenate([last, last], axis=1).astype(BF16)
        wf[1728:1792, :] = jnp.zeros((64, 128), BF16)

    def terms(g, grads, q, skip, ready):
        turned = grads.T[0:CH].astype(BF16)

        def put(t, tile):
            for r in range(4):
                t_send[g, 2 * r + t % 2, :, 128 * (t // 2) : 128 * (t // 2) + 128] = tile[
                    16 * r : 16 * r + 16
                ].astype(BF16)

        for m in range(5):
            even = jnp.dot(turned, patch(q, 2 * m, skip), preferred_element_type=F32)
            put(3 * m, even[:, 0:128])
            if m == 4:
                put(3 * m + 1, even[:, 128:256])
            else:
                odd = jnp.dot(turned, patch(q, 2 * m + 1, skip), preferred_element_type=F32)
                odd = pltpu.roll(odd, 64, 1)
                put(3 * m + 1, even[:, 128:256] + odd[:, 0:128])
                put(3 * m + 2, odd[:, 128:256])
            if m in ready:
                pair_copy(ready[m]).start()

    def part_of(buffer, u, slot):
        g, lo, hi = UNITS[u]
        return buffer.at[g, slot, :, lo:hi]

    def half_of(buffer, u, side):
        g, lo, hi = UNITS[u]
        return buffer.at[g, pl.ds(side * half, half), :, lo:hi]

    def pair_copy(u):
        return pltpu.make_async_remote_copy(
            src_ref=half_of(t_send, u, 1 - core), dst_ref=half_of(c_recv, u, 0),
            send_sem=c_ss.at[u], recv_sem=c_rs.at[u], device_id=sibling, device_id_type=MESH,
        )

    def t_copy(u, r):
        to = (mine + r) % half
        return pltpu.make_async_remote_copy(
            src_ref=part_of(t_sum, u, to), dst_ref=part_of(t_recv, u, mine),
            send_sem=t_ss.at[u, r], recv_sem=t_rs.at[u, r],
            device_id=member_id(to), device_id_type=MESH,
        )

    def z_copy(u, r):
        return pltpu.make_async_remote_copy(
            src_ref=part_of(z_recv, u, group), dst_ref=part_of(z_recv, u, group),
            send_sem=z_ss.at[u, r], recv_sem=z_rs.at[u, r],
            device_id=group_id((group + r) % groups), device_id_type=MESH,
        )

    def g_copy(u, r):
        return pltpu.make_async_remote_copy(
            src_ref=part_of(gath, u, core * half + mine), dst_ref=part_of(gath, u, core * half + mine),
            send_sem=g_ss.at[u, r], recv_sem=g_rs.at[u, r],
            device_id=member_id((mine + r) % half), device_id_type=MESH,
        )

    def f_copy(u, side):
        return pltpu.make_async_remote_copy(
            src_ref=half_of(gath, u, side), dst_ref=half_of(gath, u, side),
            send_sem=f_ss.at[u], recv_sem=f_rs.at[u], device_id=sibling, device_id_type=MESH,
        )

    def recv_of(buffer, u, slot, ss, rs, r):
        return pltpu.make_async_remote_copy(
            src_ref=part_of(buffer, u, slot), dst_ref=part_of(buffer, u, slot),
            send_sem=ss.at[u, r], recv_sem=rs.at[u, r],
            device_id=member_id((mine + 1) % half), device_id_type=MESH,
        )

    def add_up(buffer, u, count):
        g, lo, hi = UNITS[u]
        total = buffer[g, 0, :, lo:hi].astype(F32)
        for n in range(1, count):
            total = total + buffer[g, n, :, lo:hi].astype(F32)
        return total.astype(BF16)

    def scatter_start(u):
        g, lo, hi = UNITS[u]
        pair_copy(u).wait_recv()
        own = t_send[g, pl.ds(core * half, half), :, lo:hi].astype(F32)
        t_sum[g, :, :, lo:hi] = (own + c_recv[g, :, :, lo:hi].astype(F32)).astype(BF16)
        for r in range(1, half):
            t_copy(u, r).start()
        t_recv[g, mine, :, lo:hi] = t_sum[g, mine, :, lo:hi]

    def exchange_start(u):
        g, lo, hi = UNITS[u]
        for r in range(1, half):
            recv_of(t_recv, u, (mine + half - r) % half, t_ss, t_rs, r).wait_recv()
        z_recv[g, group, :, lo:hi] = add_up(t_recv, u, half)
        for r in range(1, groups):
            z_copy(u, r).start()

    def gather_start(u):
        g, lo, hi = UNITS[u]
        for r in range(1, groups):
            recv_of(z_recv, u, (group + groups - r) % groups, z_ss, z_rs, r).wait_recv()
        gath[g, core * half + mine, :, lo:hi] = add_up(z_recv, u, groups)
        for r in range(1, half):
            g_copy(u, r).start()

    def forward_start(u):
        for r in range(1, half):
            recv_of(gath, u, core * half + (mine + half - r) % half, g_ss, g_rs, r).wait_recv()
        f_copy(u, core).start()

    def gather_end(u, ref):
        g, lo, hi = UNITS[u]
        f_copy(u, 1 - core).wait_recv()
        for r in range(4):
            for t in range(2 * lo // 128, 2 * hi // 128):
                end = min(128 * t + 128, 27 * CH)
                at = 128 * (t // 2)
                ref[16 * r : 16 * r + 16, 128 * t : end] = gath[
                    g, 2 * r + t % 2, :, at : at + end - 128 * t
                ]

    def reduce_done(u):
        pair_copy(u).wait_send()
        f_copy(u, core).wait_send()
        for r in range(1, half):
            t_copy(u, r).wait_send()
            g_copy(u, r).wait_send()
        for r in range(1, groups):
            z_copy(u, r).wait_send()

    clear_halo(qp)
    loads[0].wait()
    x = dup_t(x_ref[...].astype(F32))
    field = alive(x)
    loads[1].wait()
    ct = alive(dup_t(ct_ref[...].astype(F32)))
    bricks_pack(field, ct)
    pl.semaphore_wait(barrier, total)
    halo_start(0)
    fill_own(qx, qxo, 3, field)
    xh[1 : E + 1, 1 : E + 1] = x.reshape(E, E, E, 128)
    cth[1 : E + 1, 1 : E + 1] = ct.reshape(E, E, E, 128)
    loads[2].wait()
    turn_weight(w1_ref, wt1)
    merge_weight(wt1, wn1)
    loads[3].wait()
    turn_weight(w2_ref, wt2)
    flip_weight(w2_ref, wf2)
    flip_weight(w1_ref, wf1)
    merge_weight(wt2, wn2)
    merge_weight(wf2, wm2)
    merge_weight(wf1, wm1)
    arrive(0, 0, range(4))
    arrive(0, 1, range(4))
    make_masks()
    halo_bricks()
    conv(
        wn1,
        [
            (qx, pre, 0, 12, 0, 12),
            (qxo, pre_o, 0, 2, 0, 12), (qxo, pre_o, 10, 12, 0, 12),
            (qxo, pre_o, 2, 10, 0, 2), (qxo, pre_o, 2, 10, 10, 12),
        ],
    )

    def silu(value):
        return (value * sigmoid(value)).astype(BF16).astype(F32)

    own = pre[2:10, 2:10].reshape(VOX, 128)
    act = alive(silu(own))
    fill_own(qa, qao, 2, act)
    for block, zs, ys in blocks(2):
        fill(qa, qao, block, zs, ys, silu(chosen(block, zs, ys, pre, pre_o)))
    conv(
        wn2,
        [
            (qa, sums, 0, 10, 0, 10),
            (qao, sums_o, 0, 1, 0, 10), (qao, sums_o, 9, 10, 0, 10),
            (qao, sums_o, 1, 9, 0, 1), (qao, sums_o, 1, 9, 9, 10),
        ],
    )

    def slope(value):
        sig = sigmoid(value)
        return sig, sig * (1.0 + value * (1.0 - sig))

    summed = x + sums[1:9, 1:9].reshape(VOX, 128)
    sig, steep = slope(summed)
    gs = alive(ct * steep).astype(BF16).astype(F32)
    gs_s[...] = gs
    out_ref[...] = alive(summed * sig).T[0:CH].astype(BF16)
    fill_own(qg, None, 1, gs)
    for block, zs, ys in blocks(1):
        near_sum = chosen(block, zs, ys, sums, sums_o) + xh[zs[0] : zs[1], ys[0] : ys[1]]
        near_gs = cth[zs[0] : zs[1], ys[0] : ys[1]] * slope(near_sum)[1]
        fill(qg, None, block, zs, ys, near_gs.astype(BF16).astype(F32))
    pre_s[...] = slope(own)[1]
    terms(0, gs, qa, 1, {4: 0})
    conv(wm2, [(qg, acc, 0, E, 0, E)])
    pg = alive(acc[...].reshape(VOX, 128) * pre_s[...]).astype(BF16).astype(F32)

    scatter_start(0)
    terms(1, pg, qx, 2, {2: 1, 4: 2})
    thin_pack(pg)
    scatter_start(1)
    scatter_start(2)
    halo_start(1)
    fill_own(qp, None, 1, pg)
    exchange_start(0)
    conv(wm1, [(qp, acc, 0, E, 0, E)])
    exchange_start(1)
    exchange_start(2)
    gather_start(0)
    gin = alive(gs_s[...] + conv_thin(qp, wf1))
    gather_start(1)
    gather_start(2)
    forward_start(0)
    gin_ref[...] = gin.T[0:CH].astype(BF16)
    forward_start(1)
    forward_start(2)
    for e in range(2):
        sends_done(e)
    gather_end(0, g2_ref)
    gather_end(1, g1_ref)
    gather_end(2, g1_ref)
    for u in range(3):
        reduce_done(u)


def finish(scale, out_in, gin_in, g1_in, g2_in, out_ref, gin_ref, g1_ref, g2_ref):
    out_ref[...] = out_in[...]
    gin_ref[...] = gin_in[...]
    g1_ref[...] = g1_in[...].astype(F32) * scale
    g2_ref[...] = g2_in[...].astype(F32) * scale


def body(features, cotangent, first_weight, second_weight, positions, counts):
    n_gz = lax.axis_size("gz")
    n_gy = lax.axis_size("gy")
    slots = features.shape[2]
    scale = 1.0 / math.sqrt(n_gz * n_gy * slots * VOX)
    members = PAIR * n_gy
    groups = n_gz // PAIR
    vmem = pl.BlockSpec(memory_space=pltpu.VMEM)
    smem = pl.BlockSpec(memory_space=pltpu.SMEM)
    dma = pltpu.SemaphoreType.DMA
    hbm = pl.BlockSpec(memory_space=pl.ANY)
    output, input_grad, first_sum, second_sum = pl.pallas_call(
        functools.partial(kernel, n_gz, n_gy),
        out_shape=(
            pltpu.VMEM((CH, VOX), BF16),
            pltpu.VMEM((CH, VOX), BF16),
            pltpu.VMEM((CH, 27 * CH), BF16),
            pltpu.VMEM((CH, 27 * CH), BF16),
        ),
        in_specs=[smem, smem, hbm, hbm, hbm, hbm],
        out_specs=(vmem,) * 4,
        scratch_shapes=[
            pltpu.VMEM((CH, VOX), BF16),
            pltpu.VMEM((CH, VOX), BF16),
            pltpu.VMEM((CH, 27 * CH), BF16),
            pltpu.VMEM((CH, 27 * CH), BF16),
            dma((4,)),
            pltpu.VMEM((E + 6, E + 6, E, 256), F32),
            pltpu.VMEM((E + 6, E + 6, E, 256), F32),
            pltpu.VMEM((E + 4, E + 4, E, 256), F32),
            pltpu.VMEM((E + 4, E + 4, E, 256), F32),
            pltpu.VMEM((E + 2, E + 2, E, 256), F32),
            pltpu.VMEM((E + 2, E + 2, E, 256), F32),
            pltpu.VMEM((E + 4, E + 4, E, 128), F32),
            pltpu.VMEM((E + 4, E + 4, E, 128), F32),
            pltpu.VMEM((E + 2, E + 2, E, 128), F32),
            pltpu.VMEM((E + 2, E + 2, E, 128), F32),
            pltpu.VMEM((E + 2, E + 2, E, 128), F32),
            pltpu.VMEM((E + 2, E + 2, E, 128), F32),
            pltpu.VMEM((E, E, E, 128), F32),
            pltpu.VMEM((1792, 128), BF16),
            pltpu.VMEM((1792, 128), BF16),
            pltpu.VMEM((1792, 128), BF16),
            pltpu.VMEM((1792, 128), BF16),
            pltpu.VMEM((768, 256), BF16),
            pltpu.VMEM((768, 256), BF16),
            pltpu.VMEM((768, 256), BF16),
            pltpu.VMEM((768, 256), BF16),
            pltpu.VMEM((VOX, 128), F32),
            pltpu.VMEM((VOX, 128), F32),
            pltpu.VMEM((8, E, 256), F32),
            pltpu.VMEM((8, E, 256), F32),
            pltpu.VMEM((8, E, 128), F32),
            pltpu.VMEM((4, E, 128), F32),
            pltpu.VMEM((4, 144, 128), BF16),
            pltpu.VMEM((4, 144, 128), BF16),
            pltpu.VMEM((4, 48, 128), BF16),
            pltpu.VMEM((4, 48, 128), BF16),
            pltpu.VMEM((4, 64, 128), BF16),
            pltpu.VMEM((4, 64, 128), BF16),
            pltpu.VMEM((4, 16, 128), BF16),
            pltpu.VMEM((4, 16, 128), BF16),
            pltpu.VMEM((2, members, 16, 128 * TILES), BF16),
            pltpu.VMEM((2, members // 2, 16, 128 * TILES), BF16),
            pltpu.VMEM((2, members // 2, 16, 128 * TILES), BF16),
            pltpu.VMEM((2, members // 2, 16, 128 * TILES), BF16),
            pltpu.VMEM((2, groups, 16, 128 * TILES), BF16),
            pltpu.VMEM((2, members, 16, 128 * TILES), BF16),
            dma((3,)), dma((3,)), dma((3,)), dma((3,)),
            dma((4,)), dma((4,)), dma((4,)), dma((4,)), dma((4,)), dma((4,)), dma((4,)), dma((4,)),
            dma((3, members)), dma((3, members)),
            dma((3, groups)), dma((3, groups)),
            dma((3, members)), dma((3, members)),
        ],
        compiler_params=pltpu.CompilerParams(collective_id=0, has_side_effects=True),
    )(
        positions.reshape(1), counts.reshape(1), features[0, 0, 0], cotangent[0, 0, 0],
        first_weight, second_weight,
    )
    grad = jax.ShapeDtypeStruct((CH, 27 * CH), F32)
    brick = jax.ShapeDtypeStruct((CH, VOX), BF16)
    output, input_grad, first_grad, second_grad = pl.pallas_call(
        functools.partial(finish, scale),
        out_shape=(brick, brick, grad, grad),
        in_specs=[vmem] * 4,
        out_specs=(vmem,) * 4,
    )(*(
        pltpu.with_memory_space_constraint(value, pltpu.VMEM)
        for value in (output, input_grad, first_sum, second_sum)
    ))
    return (output[None, None, None], input_grad[None, None, None], first_grad, second_grad)


def solution(mesh):
    return jax.shard_map(
        body,
        mesh=mesh,
        in_specs=(
            P("gz", "gy", None, None, None),
            P("gz", "gy", None, None, None),
            P(),
            P(),
            P("gz", "gy", None),
            P("gz", "gy"),
        ),
        out_specs=(P("gz", "gy", None, None, None), P("gz", "gy", None, None, None), P(), P()),
        check_vma=False,
    )
```

```python
import functools
import math

import jax
import jax.numpy as jnp
from jax import lax
from jax.experimental import pallas as pl
from jax.experimental.pallas import tpu as pltpu
from jax.sharding import PartitionSpec as P

E = 8
VOX = E**3
CH = 64
BX = 2
MESH = pl.DeviceIdType.MESH
F32 = jnp.float32
BF16 = jnp.bfloat16
FACES = ((-1, 0), (1, 0), (0, -1), (0, 1))
EDGES = ((-1, -1), (-1, 1), (1, -1), (1, 1))
PAIR = 4
TILES = 4
SPLIT = 4
ROWS = 256
UNITS = ((0, 0, 512), (1, 0, 256), (1, 256, 512))


def sigmoid(value):
    return 1.0 / (1.0 + jnp.exp(-value))


def kernel(
    n_gz, n_gy,
    place_ref, count_ref, x_hbm, ct_hbm, w1_hbm, w2_hbm,
    out_ref, gin_ref, g1_ref, g2_ref,
    x_ref, ct_ref, w1_ref, w2_ref, in_sems,
    qx, qxo, qa, qao, qg, qp, pre, pre_o, sums, sums_o, xh, cth, acc,
    wt1, wt2, wf1, wf2, wn1, wn2, wm1, wm2, pre_s, gs_s, masks, masks_o, same, first,
    bf_send, bf_recv, be_send, be_recv, hf_send, hf_recv, he_send, he_recv,
    t_send, c_recv, t_sum, t_recv, z_recv, gath,
    c_ss, c_rs, f_ss, f_rs, bf_ss, bf_rs, be_ss, be_rs, hf_ss, hf_rs, he_ss, he_rs, t_ss, t_rs, z_ss, z_rs, g_ss, g_rs,
):
    gz = lax.axis_index("gz")
    gy = lax.axis_index("gy")
    members = PAIR * n_gy
    groups = n_gz // PAIR
    columns = n_gy // 2
    half = members // 2
    core = gy % 2
    mine = (gz % PAIR) * columns + gy // 2
    group = gz // PAIR

    def exists(dz, dy):
        ok = None
        for pos, step, count in ((gz, dz, n_gz), (gy, dy, n_gy)):
            if step:
                here = pos + step >= 0 if step < 0 else pos + step < count
                ok = here if ok is None else jnp.logical_and(ok, here)
        return ok

    def member_id(index):
        return (group * PAIR + index // columns, (index % columns) * 2 + core)

    sibling = (gz, gy + 1 - 2 * core)

    def group_id(index):
        return (index * PAIR + gz % PAIR, gy)

    for landing in (bf_recv, be_recv, hf_recv, he_recv):
        landing[...] = jnp.zeros_like(landing)
    barrier = pltpu.get_barrier_semaphore()
    total = jnp.int32(half + groups - 1)
    for dz, dy in EDGES + FACES:
        ok = exists(dz, dy)
        total = total + ok.astype(jnp.int32)

        @pl.when(ok)
        def _(dz=dz, dy=dy):
            pl.semaphore_signal(barrier, inc=1, device_id=(gz + dz, gy + dy), device_id_type=MESH)

    pl.semaphore_signal(barrier, inc=1, device_id=sibling, device_id_type=MESH)
    for r in range(1, half):
        pl.semaphore_signal(barrier, inc=1, device_id=member_id((mine + r) % half), device_id_type=MESH)
    for r in range(1, groups):
        pl.semaphore_signal(barrier, inc=1, device_id=group_id((group + r) % groups), device_id_type=MESH)

    loads = [
        pltpu.make_async_copy(src, dst, in_sems.at[n])
        for n, (src, dst) in enumerate(
            ((x_hbm, x_ref), (ct_hbm, ct_ref), (w1_hbm, w1_ref), (w2_hbm, w2_ref))
        )
    ]
    for load in loads:
        load.start()

    place = jnp.full((E, 128), place_ref[0], jnp.int32).astype(F32)
    live = jnp.full((E, 128), count_ref[0], jnp.int32).astype(F32)
    live = jnp.where(live > 0.5, 1.0, 0.0)
    lane = lax.broadcasted_iota(jnp.int32, (E, 128), 1)
    row = lax.broadcasted_iota(jnp.int32, (E, 128), 0)
    low = lane < CH
    code = (place + 1.0) * live

    def dup_t(block):
        return jnp.concatenate([block, block], axis=0).T

    def alive(value):
        return (value.reshape(-1, E, 128) * live[None]).reshape(value.shape)

    def x3(value):
        left = pltpu.roll(value, 1, 1)
        right = pltpu.roll(value, E - 1, 1)
        first = jnp.where(low[None], left, value)
        return jnp.concatenate([first, right], axis=-1)

    def halo_copy(e, kind, index):
        offsets, sends, recvs, ss, rs = (
            ((FACES, bf_send, bf_recv, bf_ss, bf_rs), (EDGES, be_send, be_recv, be_ss, be_rs)),
            ((FACES, hf_send, hf_recv, hf_ss, hf_rs), (EDGES, he_send, he_recv, he_ss, he_rs)),
        )[e][kind]
        dz, dy = offsets[index]
        slot = offsets.index((-dz, -dy))
        return pltpu.make_async_remote_copy(
            src_ref=sends.at[index],
            dst_ref=recvs.at[slot],
            send_sem=ss.at[index],
            recv_sem=rs.at[slot],
            device_id=(gz + dz, gy + dy),
            device_id_type=MESH,
        )

    def halo_start(e):
        for kind, offsets in ((1, EDGES), (0, FACES)):
            for index, (dz, dy) in enumerate(offsets):

                @pl.when(exists(dz, dy))
                def _(kind=kind, index=index):
                    halo_copy(e, kind, index).start()

    def near(step):
        return (0, 1, 2) if step < 0 else (E - 3, E - 2, E - 1)

    def rim(step):
        return 0 if step < 0 else E - 1

    def pack(one, two):
        return jnp.where(low, one, two).astype(BF16)

    def unpack(packed):
        value = packed.astype(F32)
        turned = pltpu.roll(value, CH, value.ndim - 1)
        return jnp.where(low, value, turned), jnp.where(low, turned, value)

    def bricks_pack(x, ct):
        x = x.reshape(E, E, E, 128)
        ct = ct.reshape(E, E, E, 128)
        for index, (dz, dy) in enumerate(FACES):
            layers = [x[n] if dz else x[:, n] for n in near(dz + dy)]
            layers.append(ct[rim(dz)] if dz else ct[:, rim(dy)])
            for n in range(2):
                bf_send[index, 64 * n : 64 * n + 64, :] = pack(layers[2 * n], layers[2 * n + 1]).reshape(64, 128)
            bf_send[index, 128:144, :] = jnp.concatenate([code, code], axis=0).astype(BF16)
        for index, (dz, dy) in enumerate(EDGES):
            lines = [x[m, n] for m in near(dz) for n in near(dy)] + [ct[rim(dz), rim(dy)]]
            packed = [jnp.where(low, lines[2 * n], lines[2 * n + 1]) for n in range(5)] + [code]
            be_send[index] = jnp.concatenate(packed, axis=0).astype(BF16)

    def thin_pack(value):
        cube = value.reshape(E, E, E, 128)
        for index, (dz, dy) in enumerate(FACES):
            face = cube[rim(dz)] if dz else cube[:, rim(dy)]
            hf_send[index] = face.reshape(64, 128).astype(BF16)
        for index, (dz, dy) in enumerate(EDGES):
            edge = cube[rim(dz), rim(dy)]
            he_send[index] = jnp.concatenate([edge, edge], axis=0).astype(BF16)

    def arrive(e, kind, indices):
        offsets = (FACES, EDGES)[kind]
        for index in indices:
            dz, dy = offsets[index]

            @pl.when(exists(dz, dy))
            def _(dz=dz, dy=dy):
                halo_copy(e, kind, offsets.index((-dz, -dy))).wait_recv()

    def sends_done(e):
        for kind, offsets in ((0, FACES), (1, EDGES)):
            for index, (dz, dy) in enumerate(offsets):

                @pl.when(exists(dz, dy))
                def _(kind=kind, index=index):
                    halo_copy(e, kind, index).wait_send()

    target0 = jnp.where(jnp.logical_and(low, row == 0), -1.0, 0.0)
    target1 = jnp.where(low, jnp.where(row == E - 1, 1.0, 0.0), 99.0)

    def x_mask(delta):
        return jnp.concatenate(
            [jnp.where(delta == target0, 1.0, 0.0), jnp.where(delta == target1, 1.0, 0.0)], axis=-1
        )

    own_y = jnp.where(place >= 1.5, 1.0, 0.0)
    own_x = place - 2.0 * own_y
    own_mask = x_mask(jnp.zeros((E, 128), F32))
    own_mask_o = x_mask(2.0 * own_x - 1.0)

    def wide(mask):
        return jnp.concatenate([mask, mask], axis=-1)

    def found(theirs):
        here = jnp.where(theirs > 0.5, 1.0, 0.0)
        their_y = jnp.where(theirs >= 2.5, 1.0, 0.0)
        their_x = theirs - 1.0 - 2.0 * their_y
        return here, their_y - own_y, their_x

    def make_masks():
        def put(block, parts):
            sides = [0.0, 0.0]
            alike = 0.0
            for keep, their_x in parts:
                sides[0] = sides[0] + wide(keep) * x_mask(their_x - own_x)
                sides[1] = sides[1] + wide(keep) * x_mask(their_x - 1.0 + own_x)
                alike = alike + keep * jnp.where(their_x == own_x, 1.0, 0.0)
            masks[block] = sides[0]
            masks_o[block] = sides[1]
            same[block] = alike

        for t in range(2):
            step = 2.0 * t - 1.0
            here, by, their_x = found(bf_recv[2 + t, 128:144, :].astype(F32)[0:E])
            put(6 + t, [(here * jnp.where(2.0 * step + by == step, 1.0, 0.0), their_x)])
        for s in range(2):
            here, by, their_x = found(bf_recv[s, 128:144, :].astype(F32)[0:E])
            put(3 * s + 1, [(here * jnp.where(by == 0.0, 1.0, 0.0), their_x)])
            for t in range(2):
                step = 2.0 * t - 1.0
                keep = here * jnp.where(by == step, 1.0, 0.0)
                here_e, by_e, their_xe = found(be_recv[2 * s + t, 32:48, :].astype(F32)[E : 2 * E])
                keep_e = here_e * jnp.where(2.0 * step + by_e == step, 1.0, 0.0)
                put(3 * s + 2 * t, [(keep, their_x), (keep_e, their_xe)])
                first[2 * s + t] = keep

    def span(n, depth):
        return ((0, depth), (depth, depth + E), (depth + E, 2 * depth + E))[n]

    def blocks(depth):
        for s in range(2):
            for n in range(3):
                yield 3 * s + n, span(2 * s, depth), span(n, depth)
        for t in range(2):
            yield 6 + t, span(1, depth), span(2 * t, depth)

    def fill(q, q_o, block, zs, ys, value):
        shape = (zs[1] - zs[0], ys[1] - ys[0], E, 256)
        spread = x3(value.reshape(-1, E, 128))
        mask = own_mask if block is None else masks[block]
        q[zs[0] : zs[1], ys[0] : ys[1]] = (spread * mask[None]).reshape(shape)
        if q_o is not None:
            mask = own_mask_o if block is None else masks_o[block]
            q_o[zs[0] : zs[1], ys[0] : ys[1]] = (spread * mask[None]).reshape(shape)

    def fill_own(q, q_o, depth, value):
        fill(q, q_o, None, span(1, depth), span(1, depth), value)

    def halo_bricks():
        faces = []
        for index in range(4):
            packed = bf_recv[index, 0:128, :].reshape(2, E, E, 128)
            one, two = unpack(packed[0])
            three, ct = unpack(packed[1])
            faces.append(([one, two, three], ct))
        for t in range(2):
            layers, ct = faces[2 + t]
            at = span(2 * t, 3)[0]
            for n, layer in enumerate(layers):
                fill(qx, qxo, 6 + t, (3, 3 + E), (at + n, at + n + 1), layer.reshape(E, 1, E, 128))
            y = t * (E + 1)
            xh[1 : E + 1, y] = layers[2 if t == 0 else 0]
            cth[1 : E + 1, y] = ct
        for s in range(2):
            layers, ct = faces[s]
            at = span(2 * s, 3)[0]
            edges = []
            for t in range(2):
                one, two = unpack(be_recv[2 * s + t, 0:48, :].reshape(6, E, 128)[0:5])
                edges.append([v for n in range(5) for v in (one[n], two[n])])
            z = s * (E + 1)
            for n, layer in enumerate(layers):
                fill(qx, qxo, 3 * s + 1, (at + n, at + n + 1), (3, 3 + E), layer[None])
                for t in range(2):
                    rows = layer[near(1 - 2 * t)[0] : near(1 - 2 * t)[0] + 3]
                    edge = jnp.stack(edges[t][3 * n : 3 * n + 3])
                    corner = jnp.where((first[2 * s + t] > 0.5)[None], rows, edge)
                    y0 = span(2 * t, 3)[0]
                    fill(qx, qxo, 3 * s + 2 * t, (at + n, at + n + 1), (y0, y0 + 3), corner[None])
                    if n == (2 if s == 0 else 0):
                        xh[z, t * (E + 1)] = corner[2 if t == 0 else 0]
            xh[z, 1 : E + 1] = layers[2 if s == 0 else 0]
            cth[z, 1 : E + 1] = ct
            for t in range(2):
                cth[z, t * (E + 1)] = jnp.where(first[2 * s + t] > 0.5, ct[rim(1 - 2 * t)], edges[t][9])

    def merge_weight(w, wn):
        low256 = lax.broadcasted_iota(jnp.int32, (256, 128), 1) < CH
        for dy in range(3):
            outer = jnp.where(low256, rows_of(w, dy).astype(F32), rows_of(w, 6 + dy).astype(F32))
            wn[256 * dy : 256 * dy + 256, 0:128] = outer.astype(BF16)
            wn[256 * dy : 256 * dy + 256, 128:256] = rows_of(w, 3 + dy)

    def conv(wn, rects):
        groups, count = [[]], 0
        for q, out, z0, z1, y0, y1 in rects:
            for z in range(z0, z1 + 2):
                size = (y1 - y0) * E
                if count + size > ROWS:
                    groups.append([])
                    count = 0
                groups[-1].append((q, out, z, z0, y0, y1))
                count += size
        held = {}
        for group in groups:
            total = None
            for dy in range(3):
                rows = [q[z, y0 + dy : y1 + dy].reshape(-1, 256) for q, out, z, z0, y0, y1 in group]
                rows = jnp.concatenate(rows, axis=0).astype(BF16)
                part = jnp.dot(rows, wn[256 * dy : 256 * dy + 256, :], preferred_element_type=F32)
                total = part if total is None else total + part
            at = 0
            for q, out, z, z0, y0, y1 in group:
                size = (y1 - y0) * E
                outer = total[at : at + size, 0:128].reshape(y1 - y0, E, 128)
                inner = total[at : at + size, 128:256].reshape(y1 - y0, E, 128)
                at += size
                turned = pltpu.roll(outer, CH, 2)
                if z == z0:
                    held = {}
                held[z] = (jnp.where(low, outer, turned), inner, jnp.where(low, turned, outer))
                if z >= z0 + 2:
                    out[z - 2, y0:y1] = held[z - 2][0] + held[z - 1][1] + held[z][2]

    def chosen(block, zs, ys, here, other):
        z0, z1 = zs
        y0, y1 = ys
        return jnp.where((same[block] > 0.5)[None, None], here[z0:z1, y0:y1], other[z0:z1, y0:y1])

    def patch(q, k, skip=0):
        dz, dy = k // 3 + skip, k % 3 + skip
        return q[dz : dz + E, dy : dy + E].reshape(VOX, 256).astype(BF16)

    def clear_halo(q):
        for plane in (0, E + 1):
            q[plane] = jnp.zeros((E + 2, E, 256), F32)
            q[1 : E + 1, plane] = jnp.zeros((E, E, 256), F32)

    def rows_of(w, k):
        return w[192 * k : 192 * k + 256, :]

    def conv_thin(q, w):
        def side(pieces):
            total = None
            for piece, k in pieces:
                part = jnp.dot(piece.reshape(64, 256).astype(BF16), rows_of(w, k), preferred_element_type=F32)
                total = part if total is None else total + part
            return total.reshape(E, E, 128)

        arrive(1, 0, (2, 3))
        for t in range(2):
            spread = x3(hf_recv[2 + t].astype(F32).reshape(E, E, 128))
            q[1 : E + 1, t * (E + 1)] = spread * masks[6 + t][None]
            acc[:, t * (E - 1)] += side(
                [(q[dz : dz + E, t * (E + 1)], 3 * dz + 2 * t) for dz in range(3)]
            )
        arrive(1, 1, range(4))
        arrive(1, 0, (0, 1))
        for s in range(2):
            plane = s * (E + 1)
            face = hf_recv[s].astype(F32).reshape(E, E, 128)
            q[plane, 1 : E + 1] = x3(face) * masks[3 * s + 1][None]
            for t in range(2):
                edge = he_recv[2 * s + t].astype(F32)[0:E]
                corner = jnp.where(first[2 * s + t] > 0.5, face[rim(1 - 2 * t)], edge)
                q[plane, t * (E + 1)] = x3(corner[None])[0] * masks[3 * s + 2 * t]
            acc[s * (E - 1)] += side([(q[plane, dy : dy + E], 6 * s + dy) for dy in range(3)])
        return acc[...].reshape(VOX, 128)

    def turn_weight(w_ref, wt):
        for t in range(13):
            wt[128 * t : 128 * t + 128, :] = dup_t(w_ref[:, 128 * t : 128 * t + 128].astype(F32)).astype(BF16)
        wt[1664:1728, :] = dup_t(w_ref[:, 1664:1728].astype(F32)).astype(BF16)
        wt[1728:1792, :] = jnp.zeros((64, 128), BF16)

    def flip_weight(w_ref, wf):
        low64 = lax.broadcasted_iota(jnp.int32, (64, 128), 1) < CH
        for t in range(13):
            tile = w_ref[:, 128 * t : 128 * t + 128].astype(F32)
            turned = pltpu.roll(tile, 64, 1)
            at = (26 - 2 * t) * 64
            wf[at : at + 64, :] = jnp.where(low64, tile, turned).astype(BF16)
            wf[at - 64 : at, :] = jnp.where(low64, turned, tile).astype(BF16)
        last = w_ref[:, 1664:1728].astype(F32)
        wf[0:64, :] = jnp.concatenate([last, last], axis=1).astype(BF16)
        wf[1728:1792, :] = jnp.zeros((64, 128), BF16)

    def terms(g, grads, q, skip, ready):
        turned = grads.T[0:CH].astype(BF16)

        def put(t, tile):
            for r in range(4):
                t_send[g, SPLIT * r + t % SPLIT, :, 128 * (t // SPLIT) : 128 * (t // SPLIT) + 128] = tile[
                    16 * r : 16 * r + 16
                ].astype(BF16)

        for m in range(5):
            even = jnp.dot(turned, patch(q, 2 * m, skip), preferred_element_type=F32)
            put(3 * m, even[:, 0:128])
            if m == 4:
                put(3 * m + 1, even[:, 128:256])
            else:
                odd = jnp.dot(turned, patch(q, 2 * m + 1, skip), preferred_element_type=F32)
                odd = pltpu.roll(odd, 64, 1)
                put(3 * m + 1, even[:, 128:256] + odd[:, 0:128])
                put(3 * m + 2, odd[:, 128:256])
            if m in ready:
                pair_copy(ready[m]).start()

    def part_of(buffer, u, slot):
        g, lo, hi = UNITS[u]
        return buffer.at[g, slot, :, lo:hi]

    def half_of(buffer, u, side):
        g, lo, hi = UNITS[u]
        return buffer.at[g, pl.ds(side * half, half), :, lo:hi]

    def pair_copy(u):
        return pltpu.make_async_remote_copy(
            src_ref=half_of(t_send, u, 1 - core), dst_ref=half_of(c_recv, u, 0),
            send_sem=c_ss.at[u], recv_sem=c_rs.at[u], device_id=sibling, device_id_type=MESH,
        )

    def t_copy(u, r):
        to = (mine + r) % half
        return pltpu.make_async_remote_copy(
            src_ref=part_of(t_sum, u, to), dst_ref=part_of(t_recv, u, mine),
            send_sem=t_ss.at[u, r], recv_sem=t_rs.at[u, r],
            device_id=member_id(to), device_id_type=MESH,
        )

    def z_copy(u, r):
        return pltpu.make_async_remote_copy(
            src_ref=part_of(z_recv, u, group), dst_ref=part_of(z_recv, u, group),
            send_sem=z_ss.at[u, r], recv_sem=z_rs.at[u, r],
            device_id=group_id((group + r) % groups), device_id_type=MESH,
        )

    def g_copy(u, r):
        return pltpu.make_async_remote_copy(
            src_ref=part_of(gath, u, core * half + mine), dst_ref=part_of(gath, u, core * half + mine),
            send_sem=g_ss.at[u, r], recv_sem=g_rs.at[u, r],
            device_id=member_id((mine + r) % half), device_id_type=MESH,
        )

    def f_copy(u, side):
        return pltpu.make_async_remote_copy(
            src_ref=half_of(gath, u, side), dst_ref=half_of(gath, u, side),
            send_sem=f_ss.at[u], recv_sem=f_rs.at[u], device_id=sibling, device_id_type=MESH,
        )

    def recv_of(buffer, u, slot, ss, rs, r):
        return pltpu.make_async_remote_copy(
            src_ref=part_of(buffer, u, slot), dst_ref=part_of(buffer, u, slot),
            send_sem=ss.at[u, r], recv_sem=rs.at[u, r],
            device_id=member_id((mine + 1) % half), device_id_type=MESH,
        )

    def add_up(buffer, u, count):
        g, lo, hi = UNITS[u]
        total = buffer[g, 0, :, lo:hi].astype(F32)
        for n in range(1, count):
            total = total + buffer[g, n, :, lo:hi].astype(F32)
        return total.astype(BF16)

    def scatter_start(u):
        g, lo, hi = UNITS[u]
        pair_copy(u).wait_recv()
        own = t_send[g, pl.ds(core * half, half), :, lo:hi].astype(F32)
        t_sum[g, :, :, lo:hi] = (own + c_recv[g, :, :, lo:hi].astype(F32)).astype(BF16)
        for r in range(1, half):
            t_copy(u, r).start()
        t_recv[g, mine, :, lo:hi] = t_sum[g, mine, :, lo:hi]

    def exchange_start(u):
        g, lo, hi = UNITS[u]
        for r in range(1, half):
            recv_of(t_recv, u, (mine + half - r) % half, t_ss, t_rs, r).wait_recv()
        z_recv[g, group, :, lo:hi] = add_up(t_recv, u, half)
        for r in range(1, groups):
            z_copy(u, r).start()

    def gather_start(u):
        g, lo, hi = UNITS[u]
        for r in range(1, groups):
            recv_of(z_recv, u, (group + groups - r) % groups, z_ss, z_rs, r).wait_recv()
        gath[g, core * half + mine, :, lo:hi] = add_up(z_recv, u, groups)
        for r in range(1, half):
            g_copy(u, r).start()

    def forward_start(u):
        for r in range(1, half):
            recv_of(gath, u, core * half + (mine + half - r) % half, g_ss, g_rs, r).wait_recv()
        f_copy(u, core).start()

    def gather_end(u, ref):
        g, lo, hi = UNITS[u]
        f_copy(u, 1 - core).wait_recv()
        for r in range(4):
            for t in range(SPLIT * lo // 128, min(14, SPLIT * hi // 128)):
                end = min(128 * t + 128, 27 * CH)
                at = 128 * (t // SPLIT)
                ref[16 * r : 16 * r + 16, 128 * t : end] = gath[
                    g, SPLIT * r + t % SPLIT, :, at : at + end - 128 * t
                ]

    def reduce_done(u):
        pair_copy(u).wait_send()
        f_copy(u, core).wait_send()
        for r in range(1, half):
            t_copy(u, r).wait_send()
            g_copy(u, r).wait_send()
        for r in range(1, groups):
            z_copy(u, r).wait_send()

    for r in range(4):
        for n in range(2, SPLIT):
            t_send[:, SPLIT * r + n, :, 384:512] = jnp.zeros((2, 16, 128), BF16)
    clear_halo(qp)
    loads[0].wait()
    x = dup_t(x_ref[...].astype(F32))
    field = alive(x)
    loads[1].wait()
    ct = alive(dup_t(ct_ref[...].astype(F32)))
    bricks_pack(field, ct)
    pl.semaphore_wait(barrier, total)
    halo_start(0)
    fill_own(qx, qxo, 3, field)
    xh[1 : E + 1, 1 : E + 1] = x.reshape(E, E, E, 128)
    cth[1 : E + 1, 1 : E + 1] = ct.reshape(E, E, E, 128)
    loads[2].wait()
    turn_weight(w1_ref, wt1)
    merge_weight(wt1, wn1)
    loads[3].wait()
    turn_weight(w2_ref, wt2)
    flip_weight(w2_ref, wf2)
    flip_weight(w1_ref, wf1)
    merge_weight(wt2, wn2)
    merge_weight(wf2, wm2)
    merge_weight(wf1, wm1)
    arrive(0, 0, range(4))
    arrive(0, 1, range(4))
    make_masks()
    halo_bricks()
    conv(
        wn1,
        [
            (qx, pre, 0, 12, 0, 12),
            (qxo, pre_o, 0, 2, 0, 12), (qxo, pre_o, 10, 12, 0, 12),
            (qxo, pre_o, 2, 10, 0, 2), (qxo, pre_o, 2, 10, 10, 12),
        ],
    )

    def silu(value):
        return (value * sigmoid(value)).astype(BF16).astype(F32)

    own = pre[2:10, 2:10].reshape(VOX, 128)
    act = alive(silu(own))
    fill_own(qa, qao, 2, act)
    for block, zs, ys in blocks(2):
        fill(qa, qao, block, zs, ys, silu(chosen(block, zs, ys, pre, pre_o)))
    conv(
        wn2,
        [
            (qa, sums, 0, 10, 0, 10),
            (qao, sums_o, 0, 1, 0, 10), (qao, sums_o, 9, 10, 0, 10),
            (qao, sums_o, 1, 9, 0, 1), (qao, sums_o, 1, 9, 9, 10),
        ],
    )

    def slope(value):
        sig = sigmoid(value)
        return sig, sig * (1.0 + value * (1.0 - sig))

    summed = x + sums[1:9, 1:9].reshape(VOX, 128)
    sig, steep = slope(summed)
    gs = alive(ct * steep).astype(BF16).astype(F32)
    gs_s[...] = gs
    terms(0, gs, qa, 1, {4: 0})
    fill_own(qg, None, 1, gs)
    for block, zs, ys in blocks(1):
        near_sum = chosen(block, zs, ys, sums, sums_o) + xh[zs[0] : zs[1], ys[0] : ys[1]]
        near_gs = cth[zs[0] : zs[1], ys[0] : ys[1]] * slope(near_sum)[1]
        fill(qg, None, block, zs, ys, near_gs.astype(BF16).astype(F32))
    pre_s[...] = slope(own)[1]
    conv(wm2, [(qg, acc, 0, E, 0, E)])
    pg = alive(acc[...].reshape(VOX, 128) * pre_s[...]).astype(BF16).astype(F32)

    scatter_start(0)
    terms(1, pg, qx, 2, {2: 1, 4: 2})
    scatter_start(1)
    scatter_start(2)
    thin_pack(pg)
    out_ref[...] = alive(summed * sig).T[0:CH].astype(BF16)
    fill_own(qp, None, 1, pg)
    exchange_start(0)
    conv(wm1, [(qp, acc, 0, E, 0, E)])
    exchange_start(1)
    exchange_start(2)
    halo_start(1)
    gather_start(0)
    gather_start(1)
    gather_start(2)
    gin = alive(gs_s[...] + conv_thin(qp, wf1))
    forward_start(0)
    forward_start(1)
    forward_start(2)
    gin_ref[...] = gin.T[0:CH].astype(BF16)
    for e in range(2):
        sends_done(e)
    gather_end(0, g2_ref)
    gather_end(1, g1_ref)
    gather_end(2, g1_ref)
    for u in range(3):
        reduce_done(u)


def finish(scale, out_in, gin_in, g1_in, g2_in, out_ref, gin_ref, g1_ref, g2_ref):
    out_ref[...] = out_in[...]
    gin_ref[...] = gin_in[...]
    g1_ref[...] = g1_in[...].astype(F32) * scale
    g2_ref[...] = g2_in[...].astype(F32) * scale


def body(features, cotangent, first_weight, second_weight, positions, counts):
    n_gz = lax.axis_size("gz")
    n_gy = lax.axis_size("gy")
    slots = features.shape[2]
    scale = 1.0 / math.sqrt(n_gz * n_gy * slots * VOX)
    members = PAIR * n_gy
    groups = n_gz // PAIR
    vmem = pl.BlockSpec(memory_space=pltpu.VMEM)
    smem = pl.BlockSpec(memory_space=pltpu.SMEM)
    dma = pltpu.SemaphoreType.DMA
    hbm = pl.BlockSpec(memory_space=pl.ANY)
    output, input_grad, first_sum, second_sum = pl.pallas_call(
        functools.partial(kernel, n_gz, n_gy),
        out_shape=(
            pltpu.VMEM((CH, VOX), BF16),
            pltpu.VMEM((CH, VOX), BF16),
            pltpu.VMEM((CH, 27 * CH), BF16),
            pltpu.VMEM((CH, 27 * CH), BF16),
        ),
        in_specs=[smem, smem, hbm, hbm, hbm, hbm],
        out_specs=(vmem,) * 4,
        scratch_shapes=[
            pltpu.VMEM((CH, VOX), BF16),
            pltpu.VMEM((CH, VOX), BF16),
            pltpu.VMEM((CH, 27 * CH), BF16),
            pltpu.VMEM((CH, 27 * CH), BF16),
            dma((4,)),
            pltpu.VMEM((E + 6, E + 6, E, 256), F32),
            pltpu.VMEM((E + 6, E + 6, E, 256), F32),
            pltpu.VMEM((E + 4, E + 4, E, 256), F32),
            pltpu.VMEM((E + 4, E + 4, E, 256), F32),
            pltpu.VMEM((E + 2, E + 2, E, 256), F32),
            pltpu.VMEM((E + 2, E + 2, E, 256), F32),
            pltpu.VMEM((E + 4, E + 4, E, 128), F32),
            pltpu.VMEM((E + 4, E + 4, E, 128), F32),
            pltpu.VMEM((E + 2, E + 2, E, 128), F32),
            pltpu.VMEM((E + 2, E + 2, E, 128), F32),
            pltpu.VMEM((E + 2, E + 2, E, 128), F32),
            pltpu.VMEM((E + 2, E + 2, E, 128), F32),
            pltpu.VMEM((E, E, E, 128), F32),
            pltpu.VMEM((1792, 128), BF16),
            pltpu.VMEM((1792, 128), BF16),
            pltpu.VMEM((1792, 128), BF16),
            pltpu.VMEM((1792, 128), BF16),
            pltpu.VMEM((768, 256), BF16),
            pltpu.VMEM((768, 256), BF16),
            pltpu.VMEM((768, 256), BF16),
            pltpu.VMEM((768, 256), BF16),
            pltpu.VMEM((VOX, 128), F32),
            pltpu.VMEM((VOX, 128), F32),
            pltpu.VMEM((8, E, 256), F32),
            pltpu.VMEM((8, E, 256), F32),
            pltpu.VMEM((8, E, 128), F32),
            pltpu.VMEM((4, E, 128), F32),
            pltpu.VMEM((4, 144, 128), BF16),
            pltpu.VMEM((4, 144, 128), BF16),
            pltpu.VMEM((4, 48, 128), BF16),
            pltpu.VMEM((4, 48, 128), BF16),
            pltpu.VMEM((4, 64, 128), BF16),
            pltpu.VMEM((4, 64, 128), BF16),
            pltpu.VMEM((4, 16, 128), BF16),
            pltpu.VMEM((4, 16, 128), BF16),
            pltpu.VMEM((2, members, 16, 128 * TILES), BF16),
            pltpu.VMEM((2, members // 2, 16, 128 * TILES), BF16),
            pltpu.VMEM((2, members // 2, 16, 128 * TILES), BF16),
            pltpu.VMEM((2, members // 2, 16, 128 * TILES), BF16),
            pltpu.VMEM((2, groups, 16, 128 * TILES), BF16),
            pltpu.VMEM((2, members, 16, 128 * TILES), BF16),
            dma((3,)), dma((3,)), dma((3,)), dma((3,)),
            dma((4,)), dma((4,)), dma((4,)), dma((4,)), dma((4,)), dma((4,)), dma((4,)), dma((4,)),
            dma((3, members)), dma((3, members)),
            dma((3, groups)), dma((3, groups)),
            dma((3, members)), dma((3, members)),
        ],
        compiler_params=pltpu.CompilerParams(collective_id=0, has_side_effects=True),
    )(
        positions.reshape(1), counts.reshape(1), features[0, 0, 0], cotangent[0, 0, 0],
        first_weight, second_weight,
    )
    grad = jax.ShapeDtypeStruct((CH, 27 * CH), F32)
    brick = jax.ShapeDtypeStruct((CH, VOX), BF16)
    output, input_grad, first_grad, second_grad = pl.pallas_call(
        functools.partial(finish, scale),
        out_shape=(brick, brick, grad, grad),
        in_specs=[vmem] * 4,
        out_specs=(vmem,) * 4,
    )(*(
        pltpu.with_memory_space_constraint(value, pltpu.VMEM)
        for value in (output, input_grad, first_sum, second_sum)
    ))
    return (output[None, None, None], input_grad[None, None, None], first_grad, second_grad)


def solution(mesh):
    return jax.shard_map(
        body,
        mesh=mesh,
        in_specs=(
            P("gz", "gy", None, None, None),
            P("gz", "gy", None, None, None),
            P(),
            P(),
            P("gz", "gy", None),
            P("gz", "gy"),
        ),
        out_specs=(P("gz", "gy", None, None, None), P("gz", "gy", None, None, None), P(), P()),
        check_vma=False,
    )
```

```python
import functools
import math

import jax
import jax.numpy as jnp
from jax import lax
from jax.experimental import pallas as pl
from jax.experimental.pallas import tpu as pltpu
from jax.sharding import PartitionSpec as P

E = 8
VOX = E**3
CH = 64
BX = 2
MESH = pl.DeviceIdType.MESH
F32 = jnp.float32
BF16 = jnp.bfloat16
FACES = ((-1, 0), (1, 0), (0, -1), (0, 1))
EDGES = ((-1, -1), (-1, 1), (1, -1), (1, 1))
PAIR = 4
TILES = 4
SPLIT = 4
ROWS = 256
UNITS = ((0, 0, 512), (1, 0, 256), (1, 256, 512))


def sigmoid(value):
    return 1.0 / (1.0 + jnp.exp(-value))


def kernel(
    n_gz, n_gy,
    place_ref, count_ref, x_hbm, ct_hbm, w1_hbm, w2_hbm,
    out_ref, gin_ref, g1_ref, g2_ref,
    x_ref, ct_ref, w1_ref, w2_ref, in_sems,
    qx, qxo, qa, qao, qg, qp, pre, pre_o, sums, sums_o, xh, cth, acc,
    wt1, wt2, wf1, wf2, wn1, wn2, wm1, wm2, pre_s, gs_s, masks, masks_o, same, first,
    bf_send, bf_recv, be_send, be_recv, hf_send, hf_recv, he_send, he_recv,
    t_send, c_recv, t_sum, t_recv, z_recv, gath,
    c_ss, c_rs, f_ss, f_rs, bf_ss, bf_rs, be_ss, be_rs, hf_ss, hf_rs, he_ss, he_rs, t_ss, t_rs, z_ss, z_rs, g_ss, g_rs,
):
    gz = lax.axis_index("gz")
    gy = lax.axis_index("gy")
    members = PAIR * n_gy
    groups = n_gz // PAIR
    columns = n_gy // 2
    half = members // 2
    core = gy % 2
    mine = (gz % PAIR) * columns + gy // 2
    group = gz // PAIR

    def exists(dz, dy):
        ok = None
        for pos, step, count in ((gz, dz, n_gz), (gy, dy, n_gy)):
            if step:
                here = pos + step >= 0 if step < 0 else pos + step < count
                ok = here if ok is None else jnp.logical_and(ok, here)
        return ok

    def member_id(index):
        return (group * PAIR + index // columns, (index % columns) * 2 + core)

    sibling = (gz, gy + 1 - 2 * core)

    def group_id(index):
        return (index * PAIR + gz % PAIR, gy)

    for landing in (bf_recv, be_recv, hf_recv, he_recv):
        landing[...] = jnp.zeros_like(landing)
    barrier = pltpu.get_barrier_semaphore()
    total = jnp.int32(half + groups - 1)
    for dz, dy in EDGES + FACES:
        ok = exists(dz, dy)
        total = total + ok.astype(jnp.int32)

        @pl.when(ok)
        def _(dz=dz, dy=dy):
            pl.semaphore_signal(barrier, inc=1, device_id=(gz + dz, gy + dy), device_id_type=MESH)

    pl.semaphore_signal(barrier, inc=1, device_id=sibling, device_id_type=MESH)
    for r in range(1, half):
        pl.semaphore_signal(barrier, inc=1, device_id=member_id((mine + r) % half), device_id_type=MESH)
    for r in range(1, groups):
        pl.semaphore_signal(barrier, inc=1, device_id=group_id((group + r) % groups), device_id_type=MESH)

    loads = [
        pltpu.make_async_copy(src, dst, in_sems.at[n])
        for n, (src, dst) in enumerate(
            ((x_hbm, x_ref), (ct_hbm, ct_ref), (w1_hbm, w1_ref), (w2_hbm, w2_ref))
        )
    ]
    for load in loads:
        load.start()

    place = jnp.full((E, 128), place_ref[0], jnp.int32).astype(F32)
    live = jnp.full((E, 128), count_ref[0], jnp.int32).astype(F32)
    live = jnp.where(live > 0.5, 1.0, 0.0)
    lane = lax.broadcasted_iota(jnp.int32, (E, 128), 1)
    row = lax.broadcasted_iota(jnp.int32, (E, 128), 0)
    low = lane < CH
    code = (place + 1.0) * live

    def dup_t(block):
        return jnp.concatenate([block, block], axis=0).T

    def alive(value):
        return (value.reshape(-1, E, 128) * live[None]).reshape(value.shape)

    def x3(value):
        left = pltpu.roll(value, 1, 1)
        right = pltpu.roll(value, E - 1, 1)
        first = jnp.where(low[None], left, value)
        return jnp.concatenate([first, right], axis=-1)

    def halo_copy(e, kind, index):
        offsets, sends, recvs, ss, rs = (
            ((FACES, bf_send, bf_recv, bf_ss, bf_rs), (EDGES, be_send, be_recv, be_ss, be_rs)),
            ((FACES, hf_send, hf_recv, hf_ss, hf_rs), (EDGES, he_send, he_recv, he_ss, he_rs)),
        )[e][kind]
        dz, dy = offsets[index]
        slot = offsets.index((-dz, -dy))
        return pltpu.make_async_remote_copy(
            src_ref=sends.at[index],
            dst_ref=recvs.at[slot],
            send_sem=ss.at[index],
            recv_sem=rs.at[slot],
            device_id=(gz + dz, gy + dy),
            device_id_type=MESH,
        )

    def halo_start(e):
        for kind, offsets in ((0, FACES), (1, EDGES)):
            for index, (dz, dy) in enumerate(offsets):

                @pl.when(exists(dz, dy))
                def _(kind=kind, index=index):
                    halo_copy(e, kind, index).start()

    def near(step):
        return (0, 1, 2) if step < 0 else (E - 3, E - 2, E - 1)

    def rim(step):
        return 0 if step < 0 else E - 1

    def pack(one, two):
        return jnp.where(low, one, two).astype(BF16)

    def unpack(packed):
        value = packed.astype(F32)
        turned = pltpu.roll(value, CH, value.ndim - 1)
        return jnp.where(low, value, turned), jnp.where(low, turned, value)

    def bricks_pack(x, ct):
        x = x.reshape(E, E, E, 128)
        ct = ct.reshape(E, E, E, 128)
        for index, (dz, dy) in enumerate(FACES):
            layers = [x[n] if dz else x[:, n] for n in near(dz + dy)]
            layers.append(ct[rim(dz)] if dz else ct[:, rim(dy)])
            for n in range(2):
                bf_send[index, 64 * n : 64 * n + 64, :] = pack(layers[2 * n], layers[2 * n + 1]).reshape(64, 128)
            bf_send[index, 128:144, :] = jnp.concatenate([code, code], axis=0).astype(BF16)
        for index, (dz, dy) in enumerate(EDGES):
            lines = [x[m, n] for m in near(dz) for n in near(dy)] + [ct[rim(dz), rim(dy)]]
            packed = [jnp.where(low, lines[2 * n], lines[2 * n + 1]) for n in range(5)] + [code]
            be_send[index] = jnp.concatenate(packed, axis=0).astype(BF16)

    def thin_pack(value):
        cube = value.reshape(E, E, E, 128)
        for index, (dz, dy) in enumerate(FACES):
            face = cube[rim(dz)] if dz else cube[:, rim(dy)]
            hf_send[index] = face.reshape(64, 128).astype(BF16)
        for index, (dz, dy) in enumerate(EDGES):
            edge = cube[rim(dz), rim(dy)]
            he_send[index] = jnp.concatenate([edge, edge], axis=0).astype(BF16)

    def arrive(e, kind, indices):
        offsets = (FACES, EDGES)[kind]
        for index in indices:
            dz, dy = offsets[index]

            @pl.when(exists(dz, dy))
            def _(dz=dz, dy=dy):
                halo_copy(e, kind, offsets.index((-dz, -dy))).wait_recv()

    def sends_done(e):
        for kind, offsets in ((0, FACES), (1, EDGES)):
            for index, (dz, dy) in enumerate(offsets):

                @pl.when(exists(dz, dy))
                def _(kind=kind, index=index):
                    halo_copy(e, kind, index).wait_send()

    target0 = jnp.where(jnp.logical_and(low, row == 0), -1.0, 0.0)
    target1 = jnp.where(low, jnp.where(row == E - 1, 1.0, 0.0), 99.0)

    def x_mask(delta):
        return jnp.concatenate(
            [jnp.where(delta == target0, 1.0, 0.0), jnp.where(delta == target1, 1.0, 0.0)], axis=-1
        )

    own_y = jnp.where(place >= 1.5, 1.0, 0.0)
    own_x = place - 2.0 * own_y
    own_mask = x_mask(jnp.zeros((E, 128), F32))
    own_mask_o = x_mask(2.0 * own_x - 1.0)

    def wide(mask):
        return jnp.concatenate([mask, mask], axis=-1)

    def found(theirs):
        here = jnp.where(theirs > 0.5, 1.0, 0.0)
        their_y = jnp.where(theirs >= 2.5, 1.0, 0.0)
        their_x = theirs - 1.0 - 2.0 * their_y
        return here, their_y - own_y, their_x

    def make_masks():
        def put(block, parts):
            sides = [0.0, 0.0]
            alike = 0.0
            for keep, their_x in parts:
                sides[0] = sides[0] + wide(keep) * x_mask(their_x - own_x)
                sides[1] = sides[1] + wide(keep) * x_mask(their_x - 1.0 + own_x)
                alike = alike + keep * jnp.where(their_x == own_x, 1.0, 0.0)
            masks[block] = sides[0]
            masks_o[block] = sides[1]
            same[block] = alike

        for t in range(2):
            step = 2.0 * t - 1.0
            here, by, their_x = found(bf_recv[2 + t, 128:144, :].astype(F32)[0:E])
            put(6 + t, [(here * jnp.where(2.0 * step + by == step, 1.0, 0.0), their_x)])
        for s in range(2):
            here, by, their_x = found(bf_recv[s, 128:144, :].astype(F32)[0:E])
            put(3 * s + 1, [(here * jnp.where(by == 0.0, 1.0, 0.0), their_x)])
            for t in range(2):
                step = 2.0 * t - 1.0
                keep = here * jnp.where(by == step, 1.0, 0.0)
                here_e, by_e, their_xe = found(be_recv[2 * s + t, 32:48, :].astype(F32)[E : 2 * E])
                keep_e = here_e * jnp.where(2.0 * step + by_e == step, 1.0, 0.0)
                put(3 * s + 2 * t, [(keep, their_x), (keep_e, their_xe)])
                first[2 * s + t] = keep

    def span(n, depth):
        return ((0, depth), (depth, depth + E), (depth + E, 2 * depth + E))[n]

    def blocks(depth):
        for s in range(2):
            for n in range(3):
                yield 3 * s + n, span(2 * s, depth), span(n, depth)
        for t in range(2):
            yield 6 + t, span(1, depth), span(2 * t, depth)

    def fill(q, q_o, block, zs, ys, value):
        shape = (zs[1] - zs[0], ys[1] - ys[0], E, 256)
        spread = x3(value.reshape(-1, E, 128))
        mask = own_mask if block is None else masks[block]
        q[zs[0] : zs[1], ys[0] : ys[1]] = (spread * mask[None]).reshape(shape)
        if q_o is not None:
            mask = own_mask_o if block is None else masks_o[block]
            q_o[zs[0] : zs[1], ys[0] : ys[1]] = (spread * mask[None]).reshape(shape)

    def fill_own(q, q_o, depth, value):
        fill(q, q_o, None, span(1, depth), span(1, depth), value)

    def halo_bricks():
        faces = []
        for index in range(4):
            packed = bf_recv[index, 0:128, :].reshape(2, E, E, 128)
            one, two = unpack(packed[0])
            three, ct = unpack(packed[1])
            faces.append(([one, two, three], ct))
        for t in range(2):
            layers, ct = faces[2 + t]
            at = span(2 * t, 3)[0]
            for n, layer in enumerate(layers):
                fill(qx, qxo, 6 + t, (3, 3 + E), (at + n, at + n + 1), layer.reshape(E, 1, E, 128))
            y = t * (E + 1)
            xh[1 : E + 1, y] = layers[2 if t == 0 else 0]
            cth[1 : E + 1, y] = ct
        for s in range(2):
            layers, ct = faces[s]
            at = span(2 * s, 3)[0]
            edges = []
            for t in range(2):
                one, two = unpack(be_recv[2 * s + t, 0:48, :].reshape(6, E, 128)[0:5])
                edges.append([v for n in range(5) for v in (one[n], two[n])])
            z = s * (E + 1)
            for n, layer in enumerate(layers):
                fill(qx, qxo, 3 * s + 1, (at + n, at + n + 1), (3, 3 + E), layer[None])
                for t in range(2):
                    rows = layer[near(1 - 2 * t)[0] : near(1 - 2 * t)[0] + 3]
                    edge = jnp.stack(edges[t][3 * n : 3 * n + 3])
                    corner = jnp.where((first[2 * s + t] > 0.5)[None], rows, edge)
                    y0 = span(2 * t, 3)[0]
                    fill(qx, qxo, 3 * s + 2 * t, (at + n, at + n + 1), (y0, y0 + 3), corner[None])
                    if n == (2 if s == 0 else 0):
                        xh[z, t * (E + 1)] = corner[2 if t == 0 else 0]
            xh[z, 1 : E + 1] = layers[2 if s == 0 else 0]
            cth[z, 1 : E + 1] = ct
            for t in range(2):
                cth[z, t * (E + 1)] = jnp.where(first[2 * s + t] > 0.5, ct[rim(1 - 2 * t)], edges[t][9])

    def merge_weight(w, wn):
        low256 = lax.broadcasted_iota(jnp.int32, (256, 128), 1) < CH
        for dy in range(3):
            outer = jnp.where(low256, rows_of(w, dy).astype(F32), rows_of(w, 6 + dy).astype(F32))
            wn[256 * dy : 256 * dy + 256, 0:128] = outer.astype(BF16)
            wn[256 * dy : 256 * dy + 256, 128:256] = rows_of(w, 3 + dy)

    def conv(wn, rects):
        groups, count = [[]], 0
        for q, out, z0, z1, y0, y1 in rects:
            for z in range(z0, z1 + 2):
                size = (y1 - y0) * E
                if count + size > ROWS:
                    groups.append([])
                    count = 0
                groups[-1].append((q, out, z, z0, y0, y1))
                count += size
        held = {}
        for group in groups:
            total = None
            for dy in range(3):
                rows = [q[z, y0 + dy : y1 + dy].reshape(-1, 256) for q, out, z, z0, y0, y1 in group]
                rows = jnp.concatenate(rows, axis=0).astype(BF16)
                part = jnp.dot(rows, wn[256 * dy : 256 * dy + 256, :], preferred_element_type=F32)
                total = part if total is None else total + part
            at = 0
            for q, out, z, z0, y0, y1 in group:
                size = (y1 - y0) * E
                outer = total[at : at + size, 0:128].reshape(y1 - y0, E, 128)
                inner = total[at : at + size, 128:256].reshape(y1 - y0, E, 128)
                at += size
                turned = pltpu.roll(outer, CH, 2)
                if z == z0:
                    held = {}
                held[z] = (jnp.where(low, outer, turned), inner, jnp.where(low, turned, outer))
                if z >= z0 + 2:
                    out[z - 2, y0:y1] = held[z - 2][0] + held[z - 1][1] + held[z][2]

    def chosen(block, zs, ys, here, other):
        z0, z1 = zs
        y0, y1 = ys
        return jnp.where((same[block] > 0.5)[None, None], here[z0:z1, y0:y1], other[z0:z1, y0:y1])

    def patch(q, k, skip=0):
        dz, dy = k // 3 + skip, k % 3 + skip
        return q[dz : dz + E, dy : dy + E].reshape(VOX, 256).astype(BF16)

    def clear_halo(q):
        for plane in (0, E + 1):
            q[plane] = jnp.zeros((E + 2, E, 256), F32)
            q[1 : E + 1, plane] = jnp.zeros((E, E, 256), F32)

    def rows_of(w, k):
        return w[192 * k : 192 * k + 256, :]

    def conv_thin(q, w):
        def side(pieces):
            total = None
            for piece, k in pieces:
                part = jnp.dot(piece.reshape(64, 256).astype(BF16), rows_of(w, k), preferred_element_type=F32)
                total = part if total is None else total + part
            return total.reshape(E, E, 128)

        arrive(1, 0, (2, 3))
        for t in range(2):
            spread = x3(hf_recv[2 + t].astype(F32).reshape(E, E, 128))
            q[1 : E + 1, t * (E + 1)] = spread * masks[6 + t][None]
            acc[:, t * (E - 1)] += side(
                [(q[dz : dz + E, t * (E + 1)], 3 * dz + 2 * t) for dz in range(3)]
            )
        arrive(1, 1, range(4))
        arrive(1, 0, (0, 1))
        for s in range(2):
            plane = s * (E + 1)
            face = hf_recv[s].astype(F32).reshape(E, E, 128)
            q[plane, 1 : E + 1] = x3(face) * masks[3 * s + 1][None]
            for t in range(2):
                edge = he_recv[2 * s + t].astype(F32)[0:E]
                corner = jnp.where(first[2 * s + t] > 0.5, face[rim(1 - 2 * t)], edge)
                q[plane, t * (E + 1)] = x3(corner[None])[0] * masks[3 * s + 2 * t]
            acc[s * (E - 1)] += side([(q[plane, dy : dy + E], 6 * s + dy) for dy in range(3)])
        return acc[...].reshape(VOX, 128)

    def turn_weight(w_ref, wt):
        for t in range(13):
            wt[128 * t : 128 * t + 128, :] = dup_t(w_ref[:, 128 * t : 128 * t + 128].astype(F32)).astype(BF16)
        wt[1664:1728, :] = dup_t(w_ref[:, 1664:1728].astype(F32)).astype(BF16)
        wt[1728:1792, :] = jnp.zeros((64, 128), BF16)

    def flip_weight(w_ref, wf):
        low64 = lax.broadcasted_iota(jnp.int32, (64, 128), 1) < CH
        for t in range(13):
            tile = w_ref[:, 128 * t : 128 * t + 128].astype(F32)
            turned = pltpu.roll(tile, 64, 1)
            at = (26 - 2 * t) * 64
            wf[at : at + 64, :] = jnp.where(low64, tile, turned).astype(BF16)
            wf[at - 64 : at, :] = jnp.where(low64, turned, tile).astype(BF16)
        last = w_ref[:, 1664:1728].astype(F32)
        wf[0:64, :] = jnp.concatenate([last, last], axis=1).astype(BF16)
        wf[1728:1792, :] = jnp.zeros((64, 128), BF16)

    def terms(g, grads, q, skip, ready):
        turned = grads.T[0:CH].astype(BF16)

        def put(t, tile):
            for r in range(4):
                t_send[g, SPLIT * r + t % SPLIT, :, 128 * (t // SPLIT) : 128 * (t // SPLIT) + 128] = tile[
                    16 * r : 16 * r + 16
                ].astype(BF16)

        for m in range(5):
            even = jnp.dot(turned, patch(q, 2 * m, skip), preferred_element_type=F32)
            put(3 * m, even[:, 0:128])
            if m == 4:
                put(3 * m + 1, even[:, 128:256])
            else:
                odd = jnp.dot(turned, patch(q, 2 * m + 1, skip), preferred_element_type=F32)
                odd = pltpu.roll(odd, 64, 1)
                put(3 * m + 1, even[:, 128:256] + odd[:, 0:128])
                put(3 * m + 2, odd[:, 128:256])
            if m in ready:
                pair_copy(ready[m]).start()

    def part_of(buffer, u, slot):
        g, lo, hi = UNITS[u]
        return buffer.at[g, slot, :, lo:hi]

    def half_of(buffer, u, side):
        g, lo, hi = UNITS[u]
        return buffer.at[g, pl.ds(side * half, half), :, lo:hi]

    def pair_copy(u):
        return pltpu.make_async_remote_copy(
            src_ref=half_of(t_send, u, 1 - core), dst_ref=half_of(c_recv, u, 0),
            send_sem=c_ss.at[u], recv_sem=c_rs.at[u], device_id=sibling, device_id_type=MESH,
        )

    def t_copy(u, r):
        to = (mine + r) % half
        return pltpu.make_async_remote_copy(
            src_ref=part_of(t_sum, u, to), dst_ref=part_of(t_recv, u, mine),
            send_sem=t_ss.at[u, r], recv_sem=t_rs.at[u, r],
            device_id=member_id(to), device_id_type=MESH,
        )

    def z_copy(u, r):
        return pltpu.make_async_remote_copy(
            src_ref=part_of(z_recv, u, group), dst_ref=part_of(z_recv, u, group),
            send_sem=z_ss.at[u, r], recv_sem=z_rs.at[u, r],
            device_id=group_id((group + r) % groups), device_id_type=MESH,
        )

    def g_copy(u, r):
        return pltpu.make_async_remote_copy(
            src_ref=part_of(gath, u, core * half + mine), dst_ref=part_of(gath, u, core * half + mine),
            send_sem=g_ss.at[u, r], recv_sem=g_rs.at[u, r],
            device_id=member_id((mine + r) % half), device_id_type=MESH,
        )

    def f_copy(u, side):
        return pltpu.make_async_remote_copy(
            src_ref=half_of(gath, u, side), dst_ref=half_of(gath, u, side),
            send_sem=f_ss.at[u], recv_sem=f_rs.at[u], device_id=sibling, device_id_type=MESH,
        )

    def recv_of(buffer, u, slot, ss, rs, r):
        return pltpu.make_async_remote_copy(
            src_ref=part_of(buffer, u, slot), dst_ref=part_of(buffer, u, slot),
            send_sem=ss.at[u, r], recv_sem=rs.at[u, r],
            device_id=member_id((mine + 1) % half), device_id_type=MESH,
        )

    def add_up(buffer, u, count):
        g, lo, hi = UNITS[u]
        total = buffer[g, 0, :, lo:hi].astype(F32)
        for n in range(1, count):
            total = total + buffer[g, n, :, lo:hi].astype(F32)
        return total.astype(BF16)

    def scatter_start(u):
        g, lo, hi = UNITS[u]
        pair_copy(u).wait_recv()
        own = t_send[g, pl.ds(core * half, half), :, lo:hi].astype(F32)
        t_sum[g, :, :, lo:hi] = (own + c_recv[g, :, :, lo:hi].astype(F32)).astype(BF16)
        for r in range(1, half):
            t_copy(u, r).start()
        t_recv[g, mine, :, lo:hi] = t_sum[g, mine, :, lo:hi]

    def exchange_start(u):
        g, lo, hi = UNITS[u]
        for r in range(1, half):
            recv_of(t_recv, u, (mine + half - r) % half, t_ss, t_rs, r).wait_recv()
        z_recv[g, group, :, lo:hi] = add_up(t_recv, u, half)
        for r in range(1, groups):
            z_copy(u, r).start()

    def gather_start(u):
        g, lo, hi = UNITS[u]
        for r in range(1, groups):
            recv_of(z_recv, u, (group + groups - r) % groups, z_ss, z_rs, r).wait_recv()
        gath[g, core * half + mine, :, lo:hi] = add_up(z_recv, u, groups)
        for r in range(1, half):
            g_copy(u, r).start()

    def forward_start(u):
        for r in range(1, half):
            recv_of(gath, u, core * half + (mine + half - r) % half, g_ss, g_rs, r).wait_recv()
        f_copy(u, core).start()

    def gather_end(u, ref):
        g, lo, hi = UNITS[u]
        f_copy(u, 1 - core).wait_recv()
        for r in range(4):
            for t in range(SPLIT * lo // 128, min(14, SPLIT * hi // 128)):
                end = min(128 * t + 128, 27 * CH)
                at = 128 * (t // SPLIT)
                ref[16 * r : 16 * r + 16, 128 * t : end] = gath[
                    g, SPLIT * r + t % SPLIT, :, at : at + end - 128 * t
                ]

    def reduce_done(u):
        pair_copy(u).wait_send()
        f_copy(u, core).wait_send()
        for r in range(1, half):
            t_copy(u, r).wait_send()
            g_copy(u, r).wait_send()
        for r in range(1, groups):
            z_copy(u, r).wait_send()

    for r in range(4):
        for n in range(2, SPLIT):
            t_send[:, SPLIT * r + n, :, 384:512] = jnp.zeros((2, 16, 128), BF16)
    clear_halo(qp)
    loads[0].wait()
    x = dup_t(x_ref[...].astype(F32))
    field = alive(x)
    loads[1].wait()
    ct = alive(dup_t(ct_ref[...].astype(F32)))
    bricks_pack(field, ct)
    pl.semaphore_wait(barrier, total)
    halo_start(0)
    fill_own(qx, qxo, 3, field)
    xh[1 : E + 1, 1 : E + 1] = x.reshape(E, E, E, 128)
    cth[1 : E + 1, 1 : E + 1] = ct.reshape(E, E, E, 128)
    loads[2].wait()
    turn_weight(w1_ref, wt1)
    merge_weight(wt1, wn1)
    loads[3].wait()
    turn_weight(w2_ref, wt2)
    flip_weight(w2_ref, wf2)
    flip_weight(w1_ref, wf1)
    merge_weight(wt2, wn2)
    merge_weight(wf2, wm2)
    merge_weight(wf1, wm1)
    arrive(0, 0, range(4))
    arrive(0, 1, range(4))
    make_masks()
    halo_bricks()
    conv(
        wn1,
        [
            (qx, pre, 0, 12, 0, 12),
            (qxo, pre_o, 0, 2, 0, 12), (qxo, pre_o, 10, 12, 0, 12),
            (qxo, pre_o, 2, 10, 0, 2), (qxo, pre_o, 2, 10, 10, 12),
        ],
    )

    def silu(value):
        return (value * sigmoid(value)).astype(BF16).astype(F32)

    own = pre[2:10, 2:10].reshape(VOX, 128)
    act = alive(silu(own))
    fill_own(qa, qao, 2, act)
    for block, zs, ys in blocks(2):
        fill(qa, qao, block, zs, ys, silu(chosen(block, zs, ys, pre, pre_o)))
    conv(
        wn2,
        [
            (qa, sums, 0, 10, 0, 10),
            (qao, sums_o, 0, 1, 0, 10), (qao, sums_o, 9, 10, 0, 10),
            (qao, sums_o, 1, 9, 0, 1), (qao, sums_o, 1, 9, 9, 10),
        ],
    )

    def slope(value):
        sig = sigmoid(value)
        return sig, sig * (1.0 + value * (1.0 - sig))

    summed = x + sums[1:9, 1:9].reshape(VOX, 128)
    sig, steep = slope(summed)
    gs = alive(ct * steep).astype(BF16).astype(F32)
    gs_s[...] = gs
    terms(0, gs, qa, 1, {4: 0})
    fill_own(qg, None, 1, gs)
    for block, zs, ys in blocks(1):
        near_sum = chosen(block, zs, ys, sums, sums_o) + xh[zs[0] : zs[1], ys[0] : ys[1]]
        near_gs = cth[zs[0] : zs[1], ys[0] : ys[1]] * slope(near_sum)[1]
        fill(qg, None, block, zs, ys, near_gs.astype(BF16).astype(F32))
    pre_s[...] = slope(own)[1]
    conv(wm2, [(qg, acc, 0, E, 0, E)])
    pg = alive(acc[...].reshape(VOX, 128) * pre_s[...]).astype(BF16).astype(F32)

    scatter_start(0)
    terms(1, pg, qx, 2, {2: 1, 4: 2})
    scatter_start(1)
    scatter_start(2)
    thin_pack(pg)
    out_ref[...] = alive(summed * sig).T[0:CH].astype(BF16)
    fill_own(qp, None, 1, pg)
    exchange_start(0)
    conv(wm1, [(qp, acc, 0, E, 0, E)])
    exchange_start(1)
    exchange_start(2)
    halo_start(1)
    gather_start(0)
    gather_start(1)
    gather_start(2)
    gin = alive(gs_s[...] + conv_thin(qp, wf1))
    forward_start(0)
    forward_start(1)
    forward_start(2)
    gin_ref[...] = gin.T[0:CH].astype(BF16)
    for e in range(2):
        sends_done(e)
    gather_end(0, g2_ref)
    gather_end(1, g1_ref)
    gather_end(2, g1_ref)
    for u in range(3):
        reduce_done(u)


def finish(scale, out_in, gin_in, g1_in, g2_in, out_ref, gin_ref, g1_ref, g2_ref):
    out_ref[...] = out_in[...]
    gin_ref[...] = gin_in[...]
    g1_ref[...] = g1_in[...].astype(F32) * scale
    g2_ref[...] = g2_in[...].astype(F32) * scale


def body(features, cotangent, first_weight, second_weight, positions, counts):
    n_gz = lax.axis_size("gz")
    n_gy = lax.axis_size("gy")
    slots = features.shape[2]
    scale = 1.0 / math.sqrt(n_gz * n_gy * slots * VOX)
    members = PAIR * n_gy
    groups = n_gz // PAIR
    vmem = pl.BlockSpec(memory_space=pltpu.VMEM)
    smem = pl.BlockSpec(memory_space=pltpu.SMEM)
    dma = pltpu.SemaphoreType.DMA
    hbm = pl.BlockSpec(memory_space=pl.ANY)
    output, input_grad, first_sum, second_sum = pl.pallas_call(
        functools.partial(kernel, n_gz, n_gy),
        out_shape=(
            pltpu.VMEM((CH, VOX), BF16),
            pltpu.VMEM((CH, VOX), BF16),
            pltpu.VMEM((CH, 27 * CH), BF16),
            pltpu.VMEM((CH, 27 * CH), BF16),
        ),
        in_specs=[smem, smem, hbm, hbm, hbm, hbm],
        out_specs=(vmem,) * 4,
        scratch_shapes=[
            pltpu.VMEM((CH, VOX), BF16),
            pltpu.VMEM((CH, VOX), BF16),
            pltpu.VMEM((CH, 27 * CH), BF16),
            pltpu.VMEM((CH, 27 * CH), BF16),
            dma((4,)),
            pltpu.VMEM((E + 6, E + 6, E, 256), F32),
            pltpu.VMEM((E + 6, E + 6, E, 256), F32),
            pltpu.VMEM((E + 4, E + 4, E, 256), F32),
            pltpu.VMEM((E + 4, E + 4, E, 256), F32),
            pltpu.VMEM((E + 2, E + 2, E, 256), F32),
            pltpu.VMEM((E + 2, E + 2, E, 256), F32),
            pltpu.VMEM((E + 4, E + 4, E, 128), F32),
            pltpu.VMEM((E + 4, E + 4, E, 128), F32),
            pltpu.VMEM((E + 2, E + 2, E, 128), F32),
            pltpu.VMEM((E + 2, E + 2, E, 128), F32),
            pltpu.VMEM((E + 2, E + 2, E, 128), F32),
            pltpu.VMEM((E + 2, E + 2, E, 128), F32),
            pltpu.VMEM((E, E, E, 128), F32),
            pltpu.VMEM((1792, 128), BF16),
            pltpu.VMEM((1792, 128), BF16),
            pltpu.VMEM((1792, 128), BF16),
            pltpu.VMEM((1792, 128), BF16),
            pltpu.VMEM((768, 256), BF16),
            pltpu.VMEM((768, 256), BF16),
            pltpu.VMEM((768, 256), BF16),
            pltpu.VMEM((768, 256), BF16),
            pltpu.VMEM((VOX, 128), F32),
            pltpu.VMEM((VOX, 128), F32),
            pltpu.VMEM((8, E, 256), F32),
            pltpu.VMEM((8, E, 256), F32),
            pltpu.VMEM((8, E, 128), F32),
            pltpu.VMEM((4, E, 128), F32),
            pltpu.VMEM((4, 144, 128), BF16),
            pltpu.VMEM((4, 144, 128), BF16),
            pltpu.VMEM((4, 48, 128), BF16),
            pltpu.VMEM((4, 48, 128), BF16),
            pltpu.VMEM((4, 64, 128), BF16),
            pltpu.VMEM((4, 64, 128), BF16),
            pltpu.VMEM((4, 16, 128), BF16),
            pltpu.VMEM((4, 16, 128), BF16),
            pltpu.VMEM((2, members, 16, 128 * TILES), BF16),
            pltpu.VMEM((2, members // 2, 16, 128 * TILES), BF16),
            pltpu.VMEM((2, members // 2, 16, 128 * TILES), BF16),
            pltpu.VMEM((2, members // 2, 16, 128 * TILES), BF16),
            pltpu.VMEM((2, groups, 16, 128 * TILES), BF16),
            pltpu.VMEM((2, members, 16, 128 * TILES), BF16),
            dma((3,)), dma((3,)), dma((3,)), dma((3,)),
            dma((4,)), dma((4,)), dma((4,)), dma((4,)), dma((4,)), dma((4,)), dma((4,)), dma((4,)),
            dma((3, members)), dma((3, members)),
            dma((3, groups)), dma((3, groups)),
            dma((3, members)), dma((3, members)),
        ],
        compiler_params=pltpu.CompilerParams(collective_id=0, has_side_effects=True),
    )(
        positions.reshape(1), counts.reshape(1), features[0, 0, 0], cotangent[0, 0, 0],
        first_weight, second_weight,
    )
    grad = jax.ShapeDtypeStruct((CH, 27 * CH), F32)
    brick = jax.ShapeDtypeStruct((CH, VOX), BF16)
    output, input_grad, first_grad, second_grad = pl.pallas_call(
        functools.partial(finish, scale),
        out_shape=(brick, brick, grad, grad),
        in_specs=[vmem] * 4,
        out_specs=(vmem,) * 4,
    )(*(
        pltpu.with_memory_space_constraint(value, pltpu.VMEM)
        for value in (output, input_grad, first_sum, second_sum)
    ))
    return (output[None, None, None], input_grad[None, None, None], first_grad, second_grad)


def solution(mesh):
    return jax.shard_map(
        body,
        mesh=mesh,
        in_specs=(
            P("gz", "gy", None, None, None),
            P("gz", "gy", None, None, None),
            P(),
            P(),
            P("gz", "gy", None),
            P("gz", "gy"),
        ),
        out_specs=(P("gz", "gy", None, None, None), P("gz", "gy", None, None, None), P(), P()),
        check_vma=False,
    )
```
